256 devices in a mesh: island: 32 (over x_hi, z, core), fsdp: 8 (over y, x_lo).
Axes of the slice: x: 4 (x_hi: 2, x_lo: 2; x = x_hi * 2 + x_lo), y: 4, z: 8, core: 2. Of those that a mesh axis runs over, the one named last changes fastest.
Arguments:
- activations: bfloat16 [32768, 8192], P(('island', 'fsdp')), may hold values from -6 to 6
- cotangent: bfloat16 [32768, 1024], P(('island', 'fsdp')), may hold values from -6 to 6
- inner_weight: bfloat16 [32, 8192, 1024], P('island', 'fsdp'), may hold values from -0.125 to 0.125
- outer_weight: float32 [8192, 1024], P(('fsdp', 'island')), may hold values from -0.0625 to 0.0625
- outer_momentum: float32 [8192, 1024], P(('fsdp', 'island')), may hold values from -0.06 to 0.06
- next_activations: bfloat16 [32768, 8192], P(('island', 'fsdp')), may hold values from -6 to 6
Outputs:
- input_grad: bfloat16 [32768, 8192], P(('island', 'fsdp'))
- next_keys: bfloat16 [32768, 1024], P(('island', 'fsdp'))
- new_outer: float32 [8192, 1024], P(('fsdp', 'island'))
- new_momentum: float32 [8192, 1024], P(('fsdp', 'island'))
The draws below stay inside these ranges and needn't reach their ends.
All inputs are finite; a program needn't handle non-finite values.
Results may differ from the reference program's by a relative error of at most 0.0049.
Values may be sent and summed in bfloat16 or wider, within the bound.
A program may use at most 128 MiB of HBM per device.

```python
import jax
import jax.numpy as jnp
from jax import lax

D = 8192
KV = 1024
TOK_DEV = 128
TOKENS = 32768
N_ISLAND = 32
N_FSDP = 8


def raised(drawn, own_key, source, target, shards_of, factor):
    owner, partner = [(jnp.arange(drawn.shape[position]) // (drawn.shape[position] // shards_of)).reshape([-1 if axis == position else 1 for axis in range(drawn.ndim)]) for position in (source, target)]
    chosen = jax.random.permutation(own_key, shards_of)[partner]
    strong = (owner == chosen) | (owner == (partner + shards_of // 2) % shards_of)
    return jnp.where(strong, factor * drawn, drawn)


def levels(rng, extent, split, low, high):
    def one(dim, blocks):
        steps = jax.random.uniform(jax.random.fold_in(jax.random.fold_in(rng, 6), dim), (blocks,), jnp.float32, low / len(split), high / len(split))
        return jnp.repeat(jnp.exp(steps), extent[dim] // blocks).reshape((-1,) + (1,) * (len(extent) - dim - 1))

    loudness = one(*split[0])
    for cut in split[1:]:
        loudness = loudness * one(*cut)
    return loudness


def gaussian(key, shape, deviation, bound, split=(), kind=jnp.bfloat16):
    values = jax.random.normal(key, shape, jnp.float32) * deviation
    if len(split) > 0:
        values = levels(key, shape, split, -0.22, 0.18) * values
    return jnp.clip(values, min=-bound, max=bound).astype(kind)


def noise_with(own_key, dims, spread, reach, cuts, heavy, kind=jnp.bfloat16):
    array = spread * jax.random.normal(own_key, dims, jnp.float32)
    if cuts:
        array = array * levels(own_key, dims, cuts, -0.22, 0.18)
    return jnp.clip(raised(array, jax.random.fold_in(own_key, 3), *heavy), -reach, reach).astype(kind)


def setup_inputs(seed: int = 0) -> dict:
    arg_keys = jax.random.split(jax.random.key(seed), 7)
    return {
        "activations": gaussian(arg_keys[0], (TOKENS, D), 1.0, 6.0, ((0, 256),)),
        "cotangent": gaussian(arg_keys[1], (TOKENS, KV), 1.0, 6.0, ((0, 256),)),
        "inner_weight": noise_with(arg_keys[2], (N_ISLAND, D, KV), D ** -0.5, 0.125, ((0, 32), (1, 8)), (0, 1, 32, 2.75)),
        "outer_weight": gaussian(arg_keys[3], (D, KV), D ** -0.5, 0.0625, ((0, 256),), jnp.float32),
        "outer_momentum": gaussian(arg_keys[4], (D, KV), 0.01, 0.06, ((0, 256),), jnp.float32),
        "next_activations": gaussian(arg_keys[5], (TOKENS, D), 1.0, 6.0, ((0, 256),)),
    }


inner_rate = 1.2
outer_rate = 0.7
nesterov = 0.9


def reference(activations, cotangent, inner_weight, outer_weight, outer_momentum, next_activations):
    island_acts = activations.reshape(N_ISLAND, TOK_DEV * N_FSDP, D)
    island_cots = cotangent.reshape(N_ISLAND, TOK_DEV * N_FSDP, KV)

    def island_step(running, slices_now):
        inputs_now, cot_now, weight_now = slices_now
        weight_grad = lax.dot_general(inputs_now, cot_now, (((0,), (0,)), ((), ())), preferred_element_type=jnp.float32) / (TOK_DEV * N_FSDP)
        inner_new = weight_now.astype(jnp.float32) - inner_rate * weight_grad
        grad_rows = lax.dot_general(cot_now, weight_now, (((1,), (1,)), ((), ())), preferred_element_type=jnp.float32).astype(jnp.bfloat16)
        return running + inner_new, grad_rows

    running, grad_rows = lax.scan(island_step, jnp.zeros((D, KV), jnp.float32), (island_acts, island_cots, inner_weight))
    input_grad = grad_rows.reshape(TOKENS, D)
    pseudo_grad = outer_weight - running / N_ISLAND
    new_momentum = nesterov * outer_momentum + pseudo_grad
    new_outer = outer_weight - outer_rate * (pseudo_grad + nesterov * new_momentum)
    next_weight = new_outer.astype(jnp.bfloat16)
    next_keys = jnp.dot(next_activations, next_weight, preferred_element_type=jnp.float32).astype(jnp.bfloat16)
    return input_grad, next_keys, new_outer, new_momentum
```

```python
import jax
import jax.numpy as jnp
from jax import lax
from jax.sharding import PartitionSpec as P

inner_rate = 1.2
outer_rate = 0.7
nesterov = 0.9


def local(activations, cotangent, inner_weight, outer_weight, outer_momentum, next_activations):
    fsdp_count = lax.axis_size("fsdp")
    island_count = lax.axis_size("island")
    tok_rows = activations.shape[0]
    own_weight = inner_weight[0]
    island_cotangent = lax.all_gather(cotangent, "fsdp", axis=0, tiled=True)
    column_block = lax.all_to_all(activations, "fsdp", split_axis=1, concat_axis=0, tiled=True)
    next_block = lax.all_to_all(next_activations, "fsdp", split_axis=1, concat_axis=0, tiled=True)
    weight_grad = lax.dot_general(
        column_block, island_cotangent, (((0,), (0,)), ((), ())), preferred_element_type=jnp.float32
    ) / (tok_rows * fsdp_count)
    inner_new = own_weight.astype(jnp.float32) - inner_rate * weight_grad
    summed = lax.psum_scatter(inner_new, "island", scatter_dimension=0, tiled=True)
    grad_columns = lax.dot_general(
        island_cotangent, own_weight, (((1,), (1,)), ((), ())), preferred_element_type=jnp.float32
    ).astype(jnp.bfloat16)
    input_grad = lax.all_to_all(grad_columns, "fsdp", split_axis=0, concat_axis=1, tiled=True)
    pseudo_grad = outer_weight - summed / island_count
    new_momentum = nesterov * outer_momentum + pseudo_grad
    new_outer = outer_weight - outer_rate * (pseudo_grad + nesterov * new_momentum)
    new_share = new_outer.astype(jnp.bfloat16)
    island_block = lax.all_gather(new_share, "island", axis=0, tiled=True)
    partial = jnp.dot(next_block, island_block, preferred_element_type=jnp.float32).astype(jnp.bfloat16)
    pieces = lax.all_to_all(partial.reshape(fsdp_count, tok_rows, -1), "fsdp", split_axis=0, concat_axis=0, tiled=True)
    next_keys = jnp.sum(pieces.astype(jnp.float32), axis=0)
    return (input_grad, next_keys.astype(jnp.bfloat16), new_outer, new_momentum)


def solution(mesh):
    in_specs = (
        P(("island", "fsdp"), None),
        P(("island", "fsdp"), None),
        P("island", "fsdp", None),
        P(("fsdp", "island"), None),
        P(("fsdp", "island"), None),
        P(("island", "fsdp"), None),
    )
    out_specs = (
        P(("island", "fsdp"), None),
        P(("island", "fsdp"), None),
        P(("fsdp", "island"), None),
        P(("fsdp", "island"), None),
    )
    return jax.shard_map(local, mesh=mesh, in_specs=in_specs, out_specs=out_specs, check_vma=False)
```

```python
import functools

import jax
import jax.numpy as jnp
from jax import lax
from jax.experimental import pallas as pl
from jax.experimental.pallas import tpu as pltpu
from jax.sharding import PartitionSpec as P

inner_rate = 1.2
outer_rate = 0.7
nesterov = 0.9

TOK = 128
BLK = 1024
KV = 1024
SH = 32
F32 = jnp.float32
BF16 = jnp.bfloat16
MESH = pl.DeviceIdType.MESH


def kernel(x, g, w, ow, om, na, ig, nk, no, nm,
           wv, xr, gr, nar, igs, mine, tosib, fromsib, zs, zr, xs, xrv, nwb, ks, kr,
           loc, gss, grs, xss, xrs, nss, nrs, iss, irs, kss, krs, bss, brs, zss, zrs, hss, hrs, ass_, ars, axs, axr, sss, srs):
    isl = lax.axis_index("island")
    f = lax.axis_index("fsdp")
    core = isl % 2
    z = (isl // 2) % 8
    h = isl // 16
    yy = f // 2
    xl = f % 2

    def fdev(p):
        return {"island": isl, "fsdp": p}

    def peer(k):
        return ((yy + k // 2) % 4) * 2 + (xl + k % 2) % 2

    def source(k):
        return ((yy + 4 - k // 2) % 4) * 2 + (xl + k % 2) % 2

    sibling = {"island": h * 16 + z * 2 + 1 - core, "fsdp": f}
    partner = {"island": (1 - h) * 16 + z * 2 + core, "fsdp": f}
    zdev = [
        {"island": h * 16 + ((z + 1) % 8) * 2 + core, "fsdp": f},
        {"island": h * 16 + ((z + 7) % 8) * 2 + core, "fsdp": f},
    ]

    def cols(p):
        return pl.ds(pl.multiple_of(p * BLK, BLK), BLK)

    def rcopy(src, dst, ss, rs, dev):
        return pltpu.make_async_remote_copy(src_ref=src, dst_ref=dst, send_sem=ss, recv_sem=rs, device_id=dev, device_id_type=MESH)

    w_load = pltpu.make_async_copy(w.at[0], wv, loc.at[0])
    x_own = pltpu.make_async_copy(x.at[:, cols(f)], xr.at[f], loc.at[1])
    na_own = pltpu.make_async_copy(na.at[:, cols(f)], nar.at[f], loc.at[2])
    w_load.start()
    x_own.start()
    na_own.start()

    barrier = pltpu.get_barrier_semaphore()
    for k in range(1, 8):
        pl.semaphore_signal(barrier, inc=1, device_id=fdev(peer(k)), device_id_type=MESH)
    for dev in (sibling, partner, zdev[0], zdev[1]):
        pl.semaphore_signal(barrier, inc=1, device_id=dev, device_id_type=MESH)
    pl.semaphore_wait(barrier, 11)

    def g_copy(k):
        return rcopy(g, gr.at[f], gss.at[k], grs.at[k], fdev(peer(k)))

    def x_copy(k):
        return rcopy(x.at[:, cols(peer(k))], xr.at[f], xss.at[k], xrs.at[k], fdev(peer(k)))

    def na_copy(k):
        return rcopy(na.at[:, cols(peer(k))], nar.at[f], nss.at[k], nrs.at[k], fdev(peer(k)))

    def ig_copy(k):
        return rcopy(igs.at[source(k)], ig.at[:, cols(f)], iss.at[k], irs.at[k], fdev(source(k)))

    def key_copy(k):
        return rcopy(ks.at[source(k)], kr.at[f], kss.at[k], krs.at[k], fdev(source(k)))

    def each(body):
        lax.fori_loop(1, 8, lambda k, c: (body(k), c)[1], 0)

    each(lambda k: g_copy(k).start())
    each(lambda k: x_copy(k).start())
    each(lambda k: na_copy(k).start())
    gr[f] = g[...]

    w_load.wait()

    def grad_cols(s):
        igs[s] = lax.dot_general(gr[s], wv[...], (((1,), (1,)), ((), ())), preferred_element_type=F32).astype(BF16)

    def grad_step(k, c):
        @pl.when(k > 0)
        def _():
            g_copy(k).wait_recv()

        grad_cols(source(k))
        return c

    lax.fori_loop(0, 8, grad_step, 0)

    x_own.wait()
    each(lambda k: x_copy(k).wait_recv())

    def block_place(b):
        return b % 2, (z // 2 + 2 + b // 2) % 4

    def sib_copy(b):
        bh, bz = block_place(b)
        return rcopy(tosib.at[bh, pl.ds(bz * 2, 2)], fromsib.at[bh, pl.ds(bz * 2, 2)], bss.at[b], brs.at[b], sibling)

    def block_step(b, c):
        bh, bz = block_place(b)
        row = pl.multiple_of(bh * 512 + bz * 128, 128)
        xt = xr[:, :, pl.ds(row, 128)].reshape(8 * TOK, 128)
        grad = lax.dot_general(xt, gr[...].reshape(8 * TOK, KV), (((0,), (0,)), ((), ())), preferred_element_type=F32)
        new = wv[pl.ds(row, 128)].astype(F32) - inner_rate * (grad * (1.0 / 1024))
        new = new.reshape(2, 2, SH, KV)

        @pl.when(core == 0)
        def _():
            mine[bh, pl.ds(bz * 2, 2)] = new[:, 0]
            tosib[bh, pl.ds(bz * 2, 2)] = new[:, 1]

        @pl.when(core == 1)
        def _():
            mine[bh, pl.ds(bz * 2, 2)] = new[:, 1]
            tosib[bh, pl.ds(bz * 2, 2)] = new[:, 0]

        sib_copy(b).start()
        return c

    lax.fori_loop(0, 8, block_step, 0)
    for b in range(8):
        sib_copy(b).wait_recv()

    def z_copy(dirn, s, piece):
        return rcopy(zs.at[dirn, s, piece], zr.at[dirn, s, piece], zss.at[dirn, s, piece], zrs.at[dirn, s, piece], zdev[dirn])

    def used(dirn, s, piece):
        return s > 0 or piece == dirn

    for s in range(4):
        for piece in range(2):
            for dirn in range(2):
                if not used(dirn, s, piece):
                    continue
                t = (z + (4 - s if dirn == 0 else 4 + s)) % 8
                total = mine[piece, t] + fromsib[piece, t]
                if s > 0 and used(dirn, s - 1, piece):
                    z_copy(dirn, s - 1, piece).wait_recv()
                    total = total + zr[dirn, s - 1, piece].astype(F32)
                zs[dirn, s, piece] = total.astype(BF16)
                z_copy(dirn, s, piece).start()
    for piece in range(2):
        for dirn in range(2):
            z_copy(dirn, 3, piece).wait_recv()

    def z_total(piece):
        return mine[piece, z] + fromsib[piece, z] + zr[0, 3, piece].astype(F32) + zr[1, 3, piece].astype(F32)

    pair = rcopy(xs, xrv, hss, hrs, partner)
    xs[...] = z_total(1 - h)
    pair.start()
    own = z_total(h)
    pair.wait_recv()
    summed = own + xrv[...]
    pseudo = ow[...] - summed / 32
    momentum = nesterov * om[...] + pseudo
    outer = ow[...] - outer_rate * (pseudo + nesterov * momentum)
    nm[...] = momentum
    no[...] = outer

    def rows(ph, pz, pc):
        return pl.ds(pl.multiple_of(ph * 512 + pz * 64 + pc * 32, 32), SH)

    nwb[rows(h, z, core)] = outer.astype(BF16)

    def spread(ph, pz, ss, rs, dev):
        at = nwb.at[rows(ph, pz, core)]
        return rcopy(at, at, ss, rs, dev)

    def ring_copy(dirn, d, piece):
        pz = (z + (8 - d if dirn == 0 else d)) % 8
        return spread(piece, pz, ass_.at[dirn, d, piece], ars.at[dirn, d, piece], zdev[dirn])

    def ring_wait(dirn, d, piece):
        pz = (z + (7 - d if dirn == 0 else d + 1)) % 8
        return spread(piece, pz, ass_.at[dirn, d, piece], ars.at[dirn, d, piece], zdev[dirn]), pz

    def sib_spread(ph, pz):
        return spread(ph, pz, sss.at[ph, pz], srs.at[ph, pz], sibling)

    cross = spread(h, z, axs, axr, partner)
    cross.start()
    for dirn in range(2):
        rcopy(nwb.at[rows(h, z, core)], nwb.at[rows(h, z, core)], ass_.at[dirn, 0, h], ars.at[dirn, 0, h], zdev[dirn]).start()
    sib_spread(h, z).start()
    each(lambda k: ig_copy(k).start())
    ig_own = pltpu.make_async_copy(igs.at[f], ig.at[:, cols(f)], loc.at[3])
    ig_own.start()
    cross.wait_recv()
    for dirn in range(2):
        rcopy(nwb.at[rows(1 - h, z, core)], nwb.at[rows(1 - h, z, core)], ass_.at[dirn, 0, 1 - h], ars.at[dirn, 0, 1 - h], zdev[dirn]).start()
    sib_spread(1 - h, z).start()
    for d in range(4):
        for piece in range(2):
            for dirn in range(2):
                if d == 3 and piece != dirn:
                    continue
                arrival, pz = ring_wait(dirn, d, piece)
                arrival.wait_recv()
                last = 3 if piece == dirn else 2
                if d < last:
                    ring_copy(dirn, d + 1, piece).start()
                sib_spread(piece, pz).start()

    na_own.wait()
    each(lambda k: na_copy(k).wait_recv())
    for ph in range(2):
        for pz in range(8):
            at = nwb.at[rows(ph, pz, 1 - core)]
            rcopy(at, at, sss.at[ph, pz], srs.at[ph, pz], sibling).wait_recv()

    def key_step(k, c):
        s = source(k)
        ks[s] = jnp.dot(nar[s], nwb[...], preferred_element_type=F32).astype(BF16)
        key_copy(k).start()
        return c

    lax.fori_loop(1, 8, key_step, 0)
    keys = jnp.dot(nar[f], nwb[...], preferred_element_type=F32)
    each(lambda k: key_copy(k).wait_recv())
    nk[...] = keys

    def add_step(k, c):
        nk[...] += kr[peer(k)].astype(F32)
        return c

    lax.fori_loop(1, 8, add_step, 0)

    each(lambda k: ig_copy(k).wait_recv())
    ig_own.wait()
    for copy_of in (g_copy, x_copy, na_copy, ig_copy, key_copy):
        each(lambda k: copy_of(k).wait_send())
    for b in range(8):
        sib_copy(b).wait_send()
    for s in range(4):
        for piece in range(2):
            for dirn in range(2):
                if used(dirn, s, piece):
                    z_copy(dirn, s, piece).wait_send()
    pair.wait_send()
    cross.wait_send()
    for d in range(4):
        for piece in range(2):
            for dirn in range(2):
                if d < 3 or piece == dirn:
                    ring_copy(dirn, d, piece).wait_send()
    for ph in range(2):
        for pz in range(8):
            sib_spread(ph, pz).wait_send()


def local(activations, cotangent, inner_weight, outer_weight, outer_momentum, next_activations):
    vm = pl.BlockSpec(memory_space=pltpu.VMEM)
    hb = pl.BlockSpec(memory_space=pl.ANY)
    dma = pltpu.SemaphoreType.DMA
    ig, nk, no, nm = pl.pallas_call(
        kernel,
        out_shape=(
            jax.ShapeDtypeStruct((TOK, 8 * BLK), BF16),
            jax.ShapeDtypeStruct((TOK, KV), F32),
            jax.ShapeDtypeStruct((SH, KV), F32),
            jax.ShapeDtypeStruct((SH, KV), F32),
        ),
        in_specs=[hb, vm, hb, vm, vm, hb],
        out_specs=(hb, vm, vm, vm),
        scratch_shapes=[
            pltpu.VMEM((BLK, KV), BF16),
            pltpu.VMEM((8, TOK, BLK), BF16),
            pltpu.VMEM((8, TOK, KV), BF16),
            pltpu.VMEM((8, TOK, BLK), BF16),
            pltpu.VMEM((8, TOK, BLK), BF16),
            pltpu.VMEM((2, 8, SH, KV), F32),
            pltpu.VMEM((2, 8, SH, KV), F32),
            pltpu.VMEM((2, 8, SH, KV), F32),
            pltpu.VMEM((2, 4, 2, SH, KV), BF16),
            pltpu.VMEM((2, 4, 2, SH, KV), BF16),
            pltpu.VMEM((SH, KV), F32),
            pltpu.VMEM((SH, KV), F32),
            pltpu.VMEM((BLK, KV), BF16),
            pltpu.VMEM((8, TOK, KV), BF16),
            pltpu.VMEM((8, TOK, KV), BF16),
            dma((4,)),
            dma((8,)), dma((8,)),
            dma((8,)), dma((8,)),
            dma((8,)), dma((8,)),
            dma((8,)), dma((8,)),
            dma((8,)), dma((8,)),
            dma((8,)), dma((8,)),
            dma((2, 4, 2)), dma((2, 4, 2)),
            dma, dma,
            dma((2, 4, 2)), dma((2, 4, 2)),
            dma, dma,
            dma((2, 8)), dma((2, 8)),
        ],
        compiler_params=pltpu.CompilerParams(collective_id=0, has_side_effects=True, vmem_limit_bytes=60 * 1024 * 1024),
    )(activations, cotangent, inner_weight, outer_weight, outer_momentum, next_activations)
    return ig, nk.astype(BF16), no, nm


def solution(mesh):
    in_specs = (
        P(("island", "fsdp"), None),
        P(("island", "fsdp"), None),
        P("island", "fsdp", None),
        P(("fsdp", "island"), None),
        P(("fsdp", "island"), None),
        P(("island", "fsdp"), None),
    )
    out_specs = (
        P(("island", "fsdp"), None),
        P(("island", "fsdp"), None),
        P(("fsdp", "island"), None),
        P(("fsdp", "island"), None),
    )
    return jax.shard_map(local, mesh=mesh, in_specs=in_specs, out_specs=out_specs, check_vma=False)
```

```python
import functools

import jax
import jax.numpy as jnp
from jax import lax
from jax.experimental import pallas as pl
from jax.experimental.pallas import tpu as pltpu
from jax.sharding import PartitionSpec as P

inner_rate = 1.2
outer_rate = 0.7
nesterov = 0.9

TOK = 128
BLK = 1024
KV = 1024
SH = 32
HALF = 512
F32 = jnp.float32
BF16 = jnp.bfloat16
MESH = pl.DeviceIdType.MESH


def kernel(x, g, w, ow, om, na, ig, nk, no, nm,
           wv, xr, gr, glo, nar, igs, mine, tosib, fromsib, zs, zr, xs, xrv, nw, ksx, krx, ksy, kry, acc,
           loc, gys, gyr, gxs, gxr, xss, xrs, nss, nrs, iss, irs, kxs, kxr, kys, kyr, bss, brs, zss, zrs, hss, hrs,
           ass_, ars, axs, axr, sss, srs):
    isl = lax.axis_index("island")
    f = lax.axis_index("fsdp")
    core = isl % 2
    z = (isl // 2) % 8
    h = isl // 16
    yy = f // 2
    xl = f % 2
    across = (1 - h) * 16 + z * 2 + core

    def same(dy):
        return {"island": isl, "fsdp": ((yy + dy) % 4) * 2 + xl}

    def low(dy):
        return {"island": isl, "fsdp": ((yy + dy) % 4) * 2 + 1 - xl}

    def high(dy):
        return {"island": across, "fsdp": ((yy + dy) % 4) * 2 + 1 - xl}

    sibling = {"island": h * 16 + z * 2 + 1 - core, "fsdp": f}
    partner = {"island": across, "fsdp": f}
    zdev = [
        {"island": h * 16 + ((z + 1) % 8) * 2 + core, "fsdp": f},
        {"island": h * 16 + ((z + 7) % 8) * 2 + core, "fsdp": f},
    ]
    routes = [(same(dy), 0, TOK, yy * TOK) for dy in (1, 3, 2)]
    routes += [(low(dy), 0, 64, 512 + yy * 64) for dy in range(4)]
    routes += [(high(dy), 64, 64, 768 + yy * 64) for dy in range(4)]

    def at_rows(start, size, step):
        return pl.ds(pl.multiple_of(start, step), size)

    def cols(p):
        return at_rows(p * BLK, BLK, BLK)

    def rcopy(src, dst, ss, rs, dev):
        return pltpu.make_async_remote_copy(src_ref=src, dst_ref=dst, send_sem=ss, recv_sem=rs, device_id=dev, device_id_type=MESH)

    w_load = pltpu.make_async_copy(w.at[0], wv, loc.at[0])
    own = [pltpu.make_async_copy(x.at[:, cols(f)], xr.at[at_rows(yy * TOK, TOK, TOK)], loc.at[1]),
           pltpu.make_async_copy(na.at[:, cols(f)], nar.at[at_rows(yy * TOK, TOK, TOK)], loc.at[2])]
    w_load.start()
    own[0].start()
    own[1].start()

    barrier = pltpu.get_barrier_semaphore()
    for dev in [r[0] for r in routes] + [sibling, partner, zdev[0], zdev[1]]:
        pl.semaphore_signal(barrier, inc=1, device_id=dev, device_id_type=MESH)
    pl.semaphore_wait(barrier, 15)

    def gy_copy(n):
        return rcopy(g, gr.at[at_rows(yy * TOK, TOK, TOK)], gys.at[n], gyr.at[n], routes[n][0])

    def gx_copy(n, y):
        src = gr.at[at_rows(y * TOK + (0 if n == 0 else 64), 64, 64)]
        if n == 2:
            dst = glo.at[at_rows(y * 64, 64, 64)]
        else:
            dst = gr.at[at_rows(512 + n * 256 + y * 64, 64, 64)]
        return rcopy(src, dst, gxs.at[n, y], gxr.at[n, y], high(0) if n == 1 else low(0))

    def block_place(b):
        group = b // 2
        return b % 2, (z // 2 + (2 + group * 3 + (group // 2) * 3 + (group // 3) * 2)) % 4

    def x_copy(b, n):
        bh, bz = block_place(b)
        row = bh * 512 + bz * 128
        dev, first, size, to = routes[n]
        src = x.at[pl.ds(first, size), at_rows(dev["fsdp"] * BLK + row, 128, 128)]
        return rcopy(src, xr.at[at_rows(to, size, size), at_rows(row, 128, 128)], xss.at[b, n], xrs.at[b, n], dev)

    def na_copy(n):
        dev, first, size, to = routes[n]
        return rcopy(na.at[pl.ds(first, size), cols(dev["fsdp"])], nar.at[at_rows(to, size, size)], nss.at[n], nrs.at[n], dev)

    def ig_copy(n):
        if n < 3:
            dy = (1, 3, 2)[n]
            src, rows, dev = igs.at[at_rows(((yy + dy) % 4) * TOK, TOK, TOK)], pl.ds(0, TOK), same(dy)
        else:
            dy, half = (n - 3) % 4, (n - 3) // 4
            src, rows, dev = igs.at[at_rows(512 + half * 256 + ((yy + dy) % 4) * 64, 64, 64)], pl.ds(half * 64, 64), low(dy)
        return rcopy(src, ig.at[rows, cols(f)], iss.at[n], irs.at[n], dev)

    def send_x(b, c):
        for n in range(11):
            x_copy(b, n).start()
        return c

    for n in range(3):
        gy_copy(n).start()
    gr[at_rows(yy * TOK, TOK, TOK)] = g[...]
    for n in range(2):
        rcopy(g.at[pl.ds(n * 64, 64)], gr.at[at_rows(512 + n * 256 + yy * 64, 64, 64)], gxs.at[n, yy], gxr.at[n, yy],
              high(0) if n == 1 else low(0)).start()
    lax.fori_loop(0, 2, send_x, 0)
    for n, dy in enumerate((1, 3, 2)):
        gy_copy(n).wait_recv()
        for m in range(2):
            gx_copy(m, (yy + 4 - dy) % 4).start()
    lax.fori_loop(2, 8, send_x, 0)
    rcopy(g.at[pl.ds(64, 64)], glo.at[at_rows(yy * 64, 64, 64)], gxs.at[2, yy], gxr.at[2, yy], low(0)).start()
    for dy in (1, 3, 2):
        gx_copy(2, (yy + 4 - dy) % 4).start()

    w_load.wait()

    def grad_cols(values):
        return lax.dot_general(values, wv[...], (((1,), (1,)), ((), ())), preferred_element_type=F32).astype(BF16)

    def grad_step(k, c):
        rows = at_rows(k * TOK, TOK, TOK)
        igs[rows] = grad_cols(gr[rows])
        return c

    lax.fori_loop(0, 4, grad_step, 0)
    for m in range(2):
        for y in range(4):
            gx_copy(m, y).wait_recv()
    lax.fori_loop(4, 6, grad_step, 0)
    for n in range(3):
        na_copy(n).start()
    for n in range(3, 7):
        ig_copy(n).start()

    own[0].wait()

    def sib_copy(b):
        bh, bz = block_place(b)
        return rcopy(tosib.at[bh, pl.ds(bz * 2, 2)], fromsib.at[bh, pl.ds(bz * 2, 2)], bss.at[b], brs.at[b], sibling)

    def block_step(b, c):
        for n in range(11):
            x_copy(b, n).wait_recv()
        bh, bz = block_place(b)
        row = at_rows(bh * 512 + bz * 128, 128, 128)
        grad = lax.dot_general(xr[:, row], gr[...], (((0,), (0,)), ((), ())), preferred_element_type=F32)
        new = wv[row].astype(F32) - inner_rate * (grad * (1.0 / 1024))
        new = new.reshape(2, 2, SH, KV)

        @pl.when(core == 0)
        def _():
            mine[bh, pl.ds(bz * 2, 2)] = new[:, 0]
            tosib[bh, pl.ds(bz * 2, 2)] = new[:, 1]

        @pl.when(core == 1)
        def _():
            mine[bh, pl.ds(bz * 2, 2)] = new[:, 1]
            tosib[bh, pl.ds(bz * 2, 2)] = new[:, 0]

        sib_copy(b).start()
        return c

    def z_copy(dirn, s, piece):
        return rcopy(zs.at[dirn, s, piece], zr.at[dirn, s, piece], zss.at[dirn, s, piece], zrs.at[dirn, s, piece], zdev[dirn])

    def used(dirn, s, piece):
        return s > 0 or piece == dirn

    def ring_step(s, dirns):
        for piece in range(2):
            for dirn in dirns:
                if not used(dirn, s, piece):
                    continue
                t = (z + (4 - s if dirn == 0 else 4 + s)) % 8
                total = mine[piece, t] + fromsib[piece, t]
                if s > 0 and used(dirn, s - 1, piece):
                    z_copy(dirn, s - 1, piece).wait_recv()
                    total = total + zr[dirn, s - 1, piece].astype(F32)
                zs[dirn, s, piece] = total.astype(BF16)
                z_copy(dirn, s, piece).start()

    for group in range(4):
        lax.fori_loop(2 * group, 2 * group + 2, block_step, 0)
        for b in (2 * group, 2 * group + 1):
            sib_copy(b).wait_recv()
        if group == 0:
            ring_step(0, (0, 1))
        elif group == 1:
            ring_step(1, (0,))
        elif group == 2:
            ring_step(1, (1,))
            ring_step(2, (0, 1))
        else:
            ring_step(3, (0, 1))
    for piece in range(2):
        for dirn in range(2):
            z_copy(dirn, 3, piece).wait_recv()

    def z_total(piece):
        return mine[piece, z] + fromsib[piece, z] + zr[0, 3, piece].astype(F32) + zr[1, 3, piece].astype(F32)

    pair = rcopy(xs, xrv, hss, hrs, partner)
    xs[...] = z_total(1 - h)
    pair.start()
    own_sum = z_total(h)
    pair.wait_recv()
    summed = own_sum + xrv[...]
    pseudo = ow[...] - summed / 32
    momentum = nesterov * om[...] + pseudo
    outer = ow[...] - outer_rate * (pseudo + nesterov * momentum)
    nm[...] = momentum
    no[...] = outer

    share = outer.astype(BF16)
    for part in range(2):
        nw[part, h, z, core] = share[:, part * HALF:(part + 1) * HALF]

    def spread(part, ph, pz, ss, rs, dev):
        at = nw.at[part, ph, pz, core]
        return rcopy(at, at, ss, rs, dev)

    def ring_copy(part, dirn, d, piece):
        pz = (z + (8 - d if dirn == 0 else d)) % 8
        return spread(part, piece, pz, ass_.at[part, dirn, d, piece], ars.at[part, dirn, d, piece], zdev[dirn])

    def ring_first(part, ph):
        for dirn in range(2):
            spread(part, ph, z, ass_.at[part, dirn, 0, ph], ars.at[part, dirn, 0, ph], zdev[dirn]).start()

    def sib_spread(part, ph, pz):
        return spread(part, ph, pz, sss.at[part, ph, pz], srs.at[part, ph, pz], sibling)

    def cross(part):
        return spread(part, h, z, axs.at[part], axr.at[part], partner)

    for part in range(2):
        cross(part).start()
    for part in range(2):
        ring_first(part, h)
        sib_spread(part, h, z).start()
    for n in range(3, 11):
        na_copy(n).start()
    for part in range(2):
        cross(part).wait_recv()
        ring_first(part, 1 - h)
        sib_spread(part, 1 - h, z).start()
    for n in range(3):
        ig_copy(n).start()
    for y in range(4):
        gx_copy(2, y).wait_recv()

    def late_step(k, c):
        igs[at_rows(768 + k * TOK, TOK, TOK)] = grad_cols(glo[at_rows(k * TOK, TOK, TOK)])
        return c

    lax.fori_loop(0, 2, late_step, 0)
    for n in range(7, 9):
        ig_copy(n).start()
    ig_own = pltpu.make_async_copy(igs.at[at_rows(yy * TOK, TOK, TOK)], ig.at[:, cols(f)], loc.at[3])
    ig_own.start()

    def ring_arrival(part, d):
        for piece in range(2):
            for dirn in range(2):
                if d == 3 and piece != dirn:
                    continue
                ring_copy(part, dirn, d, piece).wait_recv()
                if d < (3 if piece == dirn else 2):
                    ring_copy(part, dirn, d + 1, piece).start()
                sib_spread(part, piece, (z + (7 - d if dirn == 0 else d + 1)) % 8).start()

    for d in range(4):
        for part in range(2):
            ring_arrival(part, d)

    def kx_copy(part, side):
        return rcopy(ksx.at[part, side], krx.at[part, side], kxs.at[part, side], kxr.at[part, side], high(0) if side else low(0))

    def ky_copy(part, n):
        dy = (1, 3, 2)[n]
        return rcopy(ksy.at[part, (yy + dy) % 4], kry.at[part, yy], kys.at[part, n], kyr.at[part, n], same(dy))

    own[1].wait()
    for n in range(11):
        na_copy(n).wait_recv()
    for part in range(2):
        for ph in range(2):
            for pz in range(8):
                sib_spread(part, ph, pz).wait_recv()
        for side in range(2):
            rows = pl.ds(512 + side * 256, 256)
            ksx[part, side] = jnp.dot(nar[rows], nw[part].reshape(BLK, HALF), preferred_element_type=F32).astype(BF16)
            kx_copy(part, side).start()
    for n in range(9, 11):
        ig_copy(n).start()
    for part in range(2):
        def own_step(y, c):
            acc[part, y] = jnp.dot(nar[at_rows(y * TOK, TOK, TOK)], nw[part].reshape(BLK, HALF), preferred_element_type=F32)
            return c

        lax.fori_loop(0, 4, own_step, 0)
    for part in range(2):
        for side in range(2):
            kx_copy(part, side).wait_recv()

        def pair_sum(y):
            other = jnp.concatenate([krx[part, 0, at_rows(y * 64, 64, 64)], krx[part, 1, at_rows(y * 64, 64, 64)]], axis=0)
            return acc[part, y] + other.astype(F32)

        for n in range(3):
            to = (yy + (1, 3, 2)[n]) % 4
            ksy[part, to] = pair_sum(to).astype(BF16)
            ky_copy(part, n).start()
        acc[part, yy] = pair_sum(yy)
    for part in range(2):
        total = acc[part, yy]
        for n in range(3):
            ky_copy(part, n).wait_recv()
            total = total + kry[part, (yy + 4 - (1, 3, 2)[n]) % 4].astype(F32)
        nk[:, pl.ds(part * HALF, HALF)] = total.astype(BF16)

    for n in range(11):
        ig_copy(n).wait_recv()
    ig_own.wait()
    for n in range(11):
        ig_copy(n).wait_send()
        na_copy(n).wait_send()
    for n in range(3):
        gy_copy(n).wait_send()
        for y in range(4):
            gx_copy(n, y).wait_send()

    def drain_x(b, c):
        for n in range(11):
            x_copy(b, n).wait_send()
        return c

    lax.fori_loop(0, 8, drain_x, 0)
    for b in range(8):
        sib_copy(b).wait_send()
    for s in range(4):
        for piece in range(2):
            for dirn in range(2):
                if used(dirn, s, piece):
                    z_copy(dirn, s, piece).wait_send()
    pair.wait_send()
    for part in range(2):
        cross(part).wait_send()
        for d in range(4):
            for piece in range(2):
                for dirn in range(2):
                    if d < 3 or piece == dirn:
                        ring_copy(part, dirn, d, piece).wait_send()
        for ph in range(2):
            for pz in range(8):
                sib_spread(part, ph, pz).wait_send()
        for side in range(2):
            kx_copy(part, side).wait_send()
        for n in range(3):
            ky_copy(part, n).wait_send()


def local(activations, cotangent, inner_weight, outer_weight, outer_momentum, next_activations):
    vm = pl.BlockSpec(memory_space=pltpu.VMEM)
    hb = pl.BlockSpec(memory_space=pl.ANY)
    dma = pltpu.SemaphoreType.DMA
    ig, nk, no, nm = pl.pallas_call(
        kernel,
        out_shape=(
            jax.ShapeDtypeStruct((TOK, 8 * BLK), BF16),
            jax.ShapeDtypeStruct((TOK, KV), BF16),
            jax.ShapeDtypeStruct((SH, KV), F32),
            jax.ShapeDtypeStruct((SH, KV), F32),
        ),
        in_specs=[hb, vm, hb, vm, vm, hb],
        out_specs=(hb, vm, vm, vm),
        scratch_shapes=[
            pltpu.VMEM((BLK, KV), BF16),
            pltpu.VMEM((8 * TOK, BLK), BF16),
            pltpu.VMEM((8 * TOK, KV), BF16),
            pltpu.VMEM((256, KV), BF16),
            pltpu.VMEM((8 * TOK, BLK), BF16),
            pltpu.VMEM((8 * TOK, BLK), BF16),
            pltpu.VMEM((2, 8, SH, KV), F32),
            pltpu.VMEM((2, 8, SH, KV), F32),
            pltpu.VMEM((2, 8, SH, KV), F32),
            pltpu.VMEM((2, 4, 2, SH, KV), BF16),
            pltpu.VMEM((2, 4, 2, SH, KV), BF16),
            pltpu.VMEM((SH, KV), F32),
            pltpu.VMEM((SH, KV), F32),
            pltpu.VMEM((2, 2, 8, 2, SH, HALF), BF16),
            pltpu.VMEM((2, 2, 256, HALF), BF16),
            pltpu.VMEM((2, 2, 256, HALF), BF16),
            pltpu.VMEM((2, 4, TOK, HALF), BF16),
            pltpu.VMEM((2, 4, TOK, HALF), BF16),
            pltpu.VMEM((2, 4, TOK, HALF), F32),
            dma((4,)),
            dma((3,)), dma((3,)),
            dma((3, 4)), dma((3, 4)),
            dma((8, 11)), dma((8, 11)),
            dma((11,)), dma((11,)),
            dma((11,)), dma((11,)),
            dma((2, 2)), dma((2, 2)),
            dma((2, 3)), dma((2, 3)),
            dma((8,)), dma((8,)),
            dma((2, 4, 2)), dma((2, 4, 2)),
            dma, dma,
            dma((2, 2, 4, 2)), dma((2, 2, 4, 2)),
            dma((2,)), dma((2,)),
            dma((2, 2, 8)), dma((2, 2, 8)),
        ],
        compiler_params=pltpu.CompilerParams(collective_id=0, has_side_effects=True, vmem_limit_bytes=60 * 1024 * 1024),
    )(activations, cotangent, inner_weight, outer_weight, outer_momentum, next_activations)
    return ig, nk, no, nm


def solution(mesh):
    in_specs = (
        P(("island", "fsdp"), None),
        P(("island", "fsdp"), None),
        P("island", "fsdp", None),
        P(("fsdp", "island"), None),
        P(("fsdp", "island"), None),
        P(("island", "fsdp"), None),
    )
    out_specs = (
        P(("island", "fsdp"), None),
        P(("island", "fsdp"), None),
        P(("fsdp", "island"), None),
        P(("fsdp", "island"), None),
    )
    return jax.shard_map(local, mesh=mesh, in_specs=in_specs, out_specs=out_specs, check_vma=False)
```

```python
import functools

import jax
import jax.numpy as jnp
from jax import lax
from jax.experimental import pallas as pl
from jax.experimental.pallas import tpu as pltpu
from jax.sharding import PartitionSpec as P

inner_rate = 1.2
outer_rate = 0.7
nesterov = 0.9

TOK = 128
BLK = 1024
KV = 1024
SH = 32
HALF = 512
QUAD = 256
XEARLY = 4
F32 = jnp.float32
BF16 = jnp.bfloat16
MESH = pl.DeviceIdType.MESH


def kernel(x, g, w, ow, om, na, ig, nk, no, nm,
           wv, xr, gr, glo, nar, igs, mine, tosib, fromsib, zs, zr, xs, xrv, nw, ksx, krx, ksy, kry, acc,
           loc, gys, gyr, gxs, gxr, xss, xrs, nss, nrs, iss, irs, kxs, kxr, kys, kyr, bss, brs, zss, zrs, hss, hrs,
           ass_, ars, axs, axr, sss, srs):
    isl = lax.axis_index("island")
    f = lax.axis_index("fsdp")
    core = isl % 2
    z = (isl // 2) % 8
    h = isl // 16
    yy = f // 2
    xl = f % 2
    across = (1 - h) * 16 + z * 2 + core

    def same(dy):
        return {"island": isl, "fsdp": ((yy + dy) % 4) * 2 + xl}

    def low(dy):
        return {"island": isl, "fsdp": ((yy + dy) % 4) * 2 + 1 - xl}

    def high(dy):
        return {"island": across, "fsdp": ((yy + dy) % 4) * 2 + 1 - xl}

    sibling = {"island": h * 16 + z * 2 + 1 - core, "fsdp": f}
    partner = {"island": across, "fsdp": f}
    zdev = [
        {"island": h * 16 + ((z + 1) % 8) * 2 + core, "fsdp": f},
        {"island": h * 16 + ((z + 7) % 8) * 2 + core, "fsdp": f},
    ]
    routes = [(same(dy), 0, TOK, yy * TOK) for dy in (1, 3, 2)]
    routes += [(low(dy), 0, 64, 512 + yy * 64) for dy in range(4)]
    routes += [(high(dy), 64, 64, 768 + yy * 64) for dy in range(4)]

    def at_rows(start, size, step):
        return pl.ds(pl.multiple_of(start, step), size)

    def cols(p):
        return at_rows(p * BLK, BLK, BLK)

    def rcopy(src, dst, ss, rs, dev):
        return pltpu.make_async_remote_copy(src_ref=src, dst_ref=dst, send_sem=ss, recv_sem=rs, device_id=dev, device_id_type=MESH)

    w_load = pltpu.make_async_copy(w.at[0], wv, loc.at[0])
    own = [pltpu.make_async_copy(x.at[:, cols(f)], xr.at[at_rows(yy * TOK, TOK, TOK)], loc.at[1]),
           pltpu.make_async_copy(na.at[:, cols(f)], nar.at[at_rows(yy * TOK, TOK, TOK)], loc.at[2])]
    w_load.start()
    own[0].start()
    own[1].start()

    barrier = pltpu.get_barrier_semaphore()
    for dev in [r[0] for r in routes] + [sibling, partner, zdev[0], zdev[1]]:
        pl.semaphore_signal(barrier, inc=1, device_id=dev, device_id_type=MESH)
    pl.semaphore_wait(barrier, 15)

    def gy_copy(n):
        return rcopy(g, gr.at[at_rows(yy * TOK, TOK, TOK)], gys.at[n], gyr.at[n], routes[n][0])

    def gx_copy(n, y):
        src = gr.at[at_rows(y * TOK + (0 if n == 0 else 64), 64, 64)]
        if n == 2:
            dst = glo.at[at_rows(y * 64, 64, 64)]
        else:
            dst = gr.at[at_rows(512 + n * 256 + y * 64, 64, 64)]
        return rcopy(src, dst, gxs.at[n, y], gxr.at[n, y], high(0) if n == 1 else low(0))

    def block_place(b):
        group = b // 2
        return (1 - h + b) % 2, (z // 2 + (2 + group * 3 + (group // 2) * 3 + (group // 3) * 2)) % 4

    def x_copy(b, n):
        bh, bz = block_place(b)
        if n >= 7:
            bh = 1 - bh
        row = bh * 512 + bz * 128
        dev, first, size, to = routes[n]
        src = x.at[pl.ds(first, size), at_rows(dev["fsdp"] * BLK + row, 128, 128)]
        return rcopy(src, xr.at[at_rows(to, size, size), at_rows(row, 128, 128)], xss.at[b, n], xrs.at[b, n], dev)

    def na_copy(n):
        dev, first, size, to = routes[n]
        return rcopy(na.at[pl.ds(first, size), cols(dev["fsdp"])], nar.at[at_rows(to, size, size)], nss.at[n], nrs.at[n], dev)

    def ig_copy(n):
        if n < 3:
            dy = (1, 3, 2)[n]
            src, rows, dev = igs.at[at_rows(((yy + dy) % 4) * TOK, TOK, TOK)], pl.ds(0, TOK), same(dy)
        else:
            dy, half = (n - 3) % 4, (n - 3) // 4
            src, rows, dev = igs.at[at_rows(512 + half * 256 + ((yy + dy) % 4) * 64, 64, 64)], pl.ds(half * 64, 64), low(dy)
        return rcopy(src, ig.at[rows, cols(f)], iss.at[n], irs.at[n], dev)

    def send_x(routed):
        def body(b, c):
            for n in routed:
                x_copy(b, n).start()
            return c

        return body

    for n in range(3):
        gy_copy(n).start()
    gr[at_rows(yy * TOK, TOK, TOK)] = g[...]
    for n in range(2):
        rcopy(g.at[pl.ds(n * 64, 64)], gr.at[at_rows(512 + n * 256 + yy * 64, 64, 64)], gxs.at[n, yy], gxr.at[n, yy],
              high(0) if n == 1 else low(0)).start()
    lax.fori_loop(0, XEARLY, send_x(range(3)), 0)
    for n, dy in enumerate((1, 3, 2)):
        gy_copy(n).wait_recv()
        for m in range(2):
            gx_copy(m, (yy + 4 - dy) % 4).start()
    lax.fori_loop(0, XEARLY, send_x(range(3, 11)), 0)
    lax.fori_loop(XEARLY, 8, send_x(range(11)), 0)
    rcopy(g.at[pl.ds(64, 64)], glo.at[at_rows(yy * 64, 64, 64)], gxs.at[2, yy], gxr.at[2, yy], low(0)).start()
    for dy in (1, 3, 2):
        gx_copy(2, (yy + 4 - dy) % 4).start()

    w_load.wait()

    def grad_cols(values):
        return lax.dot_general(values, wv[...], (((1,), (1,)), ((), ())), preferred_element_type=F32).astype(BF16)

    def grad_step(k, c):
        rows = at_rows(k * TOK, TOK, TOK)
        igs[rows] = grad_cols(gr[rows])
        return c

    lax.fori_loop(0, 4, grad_step, 0)
    for m in range(2):
        for y in range(4):
            gx_copy(m, y).wait_recv()
    lax.fori_loop(4, 6, grad_step, 0)
    for n in range(3):
        na_copy(n).start()
    for n in range(3, 7):
        ig_copy(n).start()

    own[0].wait()

    def sib_copy(b):
        bh, bz = block_place(b)
        return rcopy(tosib.at[bh, pl.ds(bz * 2, 2)], fromsib.at[bh, pl.ds(bz * 2, 2)], bss.at[b], brs.at[b], sibling)

    def block_step(b, c):
        for n in range(11):
            x_copy(b, n).wait_recv()
        bh, bz = block_place(b)
        row = at_rows(bh * 512 + bz * 128, 128, 128)
        grad = lax.dot_general(xr[:, row], gr[...], (((0,), (0,)), ((), ())), preferred_element_type=F32)
        new = wv[row].astype(F32) - inner_rate * (grad * (1.0 / 1024))
        new = new.reshape(2, 2, SH, KV)

        @pl.when(core == 0)
        def _():
            mine[bh, pl.ds(bz * 2, 2)] = new[:, 0]
            tosib[bh, pl.ds(bz * 2, 2)] = new[:, 1]

        @pl.when(core == 1)
        def _():
            mine[bh, pl.ds(bz * 2, 2)] = new[:, 1]
            tosib[bh, pl.ds(bz * 2, 2)] = new[:, 0]

        sib_copy(b).start()
        return c

    def z_copy(dirn, s, piece):
        return rcopy(zs.at[dirn, s, piece], zr.at[dirn, s, piece], zss.at[dirn, s, piece], zrs.at[dirn, s, piece], zdev[dirn])

    def used(dirn, s, piece):
        return s > 0 or piece == dirn

    def plane(piece):
        return h if piece else 1 - h

    def ring_step(s, dirns, piece):
        for dirn in dirns:
            if not used(dirn, s, piece):
                continue
            t = (z + (4 - s if dirn == 0 else 4 + s)) % 8
            total = mine[plane(piece), t] + fromsib[plane(piece), t]
            if s > 0 and used(dirn, s - 1, piece):
                z_copy(dirn, s - 1, piece).wait_recv()
                total = total + zr[dirn, s - 1, piece].astype(F32)
            zs[dirn, s, piece] = total.astype(BF16)
            z_copy(dirn, s, piece).start()

    for group in range(4):
        lax.fori_loop(2 * group, 2 * group + 2, block_step, 0)
        s, dirns = ((0, (0, 1)), (1, (0,)), (1, (1,)), (3, (0, 1)))[group]
        for piece in range(2):
            sib_copy(2 * group + piece).wait_recv()
            ring_step(s, dirns, piece)
        if group == 2:
            for piece in range(2):
                ring_step(2, (0, 1), piece)

    def z_total(piece):
        for dirn in range(2):
            z_copy(dirn, 3, piece).wait_recv()
        at = plane(piece)
        return mine[at, z] + fromsib[at, z] + zr[0, 3, piece].astype(F32) + zr[1, 3, piece].astype(F32)

    pair = rcopy(xs, xrv, hss, hrs, partner)
    xs[...] = z_total(0)
    pair.start()
    own_sum = z_total(1)
    pair.wait_recv()
    summed = own_sum + xrv[...]
    pseudo = ow[...] - summed / 32
    momentum = nesterov * om[...] + pseudo
    outer = ow[...] - outer_rate * (pseudo + nesterov * momentum)
    nm[...] = momentum
    no[...] = outer

    share = outer.astype(BF16)
    for part in range(2):
        nw[part, h, z, core] = share[:, part * HALF:(part + 1) * HALF]

    def spread(part, ph, pz, ss, rs, dev):
        at = nw.at[part, ph, pz, core]
        return rcopy(at, at, ss, rs, dev)

    def ring_copy(part, dirn, d, piece):
        pz = (z + (8 - d if dirn == 0 else d)) % 8
        return spread(part, piece, pz, ass_.at[part, dirn, d, piece], ars.at[part, dirn, d, piece], zdev[dirn])

    def ring_first(part, ph):
        for dirn in range(2):
            spread(part, ph, z, ass_.at[part, dirn, 0, ph], ars.at[part, dirn, 0, ph], zdev[dirn]).start()

    def sib_spread(part, ph, pz):
        return spread(part, ph, pz, sss.at[part, ph, pz], srs.at[part, ph, pz], sibling)

    def cross(part):
        return spread(part, h, z, axs.at[part], axr.at[part], partner)

    for part in range(2):
        cross(part).start()
    for part in range(2):
        ring_first(part, h)
        sib_spread(part, h, z).start()
    for n in range(3, 11):
        na_copy(n).start()
    for part in range(2):
        cross(part).wait_recv()
        ring_first(part, 1 - h)
        sib_spread(part, 1 - h, z).start()
    for n in range(3):
        ig_copy(n).start()
    for y in range(4):
        gx_copy(2, y).wait_recv()

    def late_step(k, c):
        igs[at_rows(768 + k * TOK, TOK, TOK)] = grad_cols(glo[at_rows(k * TOK, TOK, TOK)])
        return c

    lax.fori_loop(0, 2, late_step, 0)
    for n in range(7, 9):
        ig_copy(n).start()
    ig_own = pltpu.make_async_copy(igs.at[at_rows(yy * TOK, TOK, TOK)], ig.at[:, cols(f)], loc.at[3])
    ig_own.start()

    def ring_arrival(part, d):
        for piece in range(2):
            for dirn in range(2):
                if d == 3 and piece != dirn:
                    continue
                ring_copy(part, dirn, d, piece).wait_recv()
                if d < (3 if piece == dirn else 2):
                    ring_copy(part, dirn, d + 1, piece).start()
                sib_spread(part, piece, (z + (7 - d if dirn == 0 else d + 1)) % 8).start()

    for d in range(4):
        for part in range(2):
            ring_arrival(part, d)

    def kx_copy(q, side):
        return rcopy(ksx.at[q, side], krx.at[q, side], kxs.at[q, side], kxr.at[q, side], high(0) if side else low(0))

    def ky_copy(q, n):
        dy = (1, 3, 2)[n]
        return rcopy(ksy.at[q, (yy + dy) % 4], kry.at[q, yy], kys.at[q, n], kyr.at[q, n], same(dy))

    def weight(q):
        return nw[q // 2, :, :, :, :, pl.ds(q % 2 * QUAD, QUAD)].reshape(BLK, QUAD)

    own[1].wait()
    for n in range(11):
        na_copy(n).wait_recv()
    for q in range(4):
        if q % 2 == 0:
            for ph in range(2):
                for pz in range(8):
                    sib_spread(q // 2, ph, pz).wait_recv()
        for side in range(2):
            ksx[q, side] = jnp.dot(nar[pl.ds(512 + side * 256, 256)], weight(q), preferred_element_type=F32).astype(BF16)
            kx_copy(q, side).start()
    for n in range(9, 11):
        ig_copy(n).start()
    for q in range(4):
        acc[q] = jnp.dot(nar[pl.ds(0, 512)], weight(q), preferred_element_type=F32).reshape(4, TOK, QUAD)
    for q in range(4):
        for side in range(2):
            kx_copy(q, side).wait_recv()

        def pair_sum(y):
            other = jnp.concatenate([krx[q, 0, at_rows(y * 64, 64, 64)], krx[q, 1, at_rows(y * 64, 64, 64)]], axis=0)
            return acc[q, y] + other.astype(F32)

        for n in range(3):
            to = (yy + (1, 3, 2)[n]) % 4
            ksy[q, to] = pair_sum(to).astype(BF16)
            ky_copy(q, n).start()
        acc[q, yy] = pair_sum(yy)
    for q in range(4):
        total = acc[q, yy]
        for n in range(3):
            ky_copy(q, n).wait_recv()
            total = total + kry[q, (yy + 4 - (1, 3, 2)[n]) % 4].astype(F32)
        nk[:, pl.ds(q * QUAD, QUAD)] = total.astype(BF16)

    for n in range(11):
        ig_copy(n).wait_recv()
    ig_own.wait()
    for n in range(11):
        ig_copy(n).wait_send()
        na_copy(n).wait_send()
    for n in range(3):
        gy_copy(n).wait_send()
        for y in range(4):
            gx_copy(n, y).wait_send()

    def drain_x(b, c):
        for n in range(11):
            x_copy(b, n).wait_send()
        return c

    lax.fori_loop(0, 8, drain_x, 0)
    for b in range(8):
        sib_copy(b).wait_send()
    for s in range(4):
        for piece in range(2):
            for dirn in range(2):
                if used(dirn, s, piece):
                    z_copy(dirn, s, piece).wait_send()
    pair.wait_send()
    for part in range(2):
        cross(part).wait_send()
        for d in range(4):
            for piece in range(2):
                for dirn in range(2):
                    if d < 3 or piece == dirn:
                        ring_copy(part, dirn, d, piece).wait_send()
        for ph in range(2):
            for pz in range(8):
                sib_spread(part, ph, pz).wait_send()
    for q in range(4):
        for side in range(2):
            kx_copy(q, side).wait_send()
        for n in range(3):
            ky_copy(q, n).wait_send()


def local(activations, cotangent, inner_weight, outer_weight, outer_momentum, next_activations):
    vm = pl.BlockSpec(memory_space=pltpu.VMEM)
    hb = pl.BlockSpec(memory_space=pl.ANY)
    dma = pltpu.SemaphoreType.DMA
    ig, nk, no, nm = pl.pallas_call(
        kernel,
        out_shape=(
            jax.ShapeDtypeStruct((TOK, 8 * BLK), BF16),
            jax.ShapeDtypeStruct((TOK, KV), BF16),
            jax.ShapeDtypeStruct((SH, KV), F32),
            jax.ShapeDtypeStruct((SH, KV), F32),
        ),
        in_specs=[hb, vm, hb, vm, vm, hb],
        out_specs=(hb, vm, vm, vm),
        scratch_shapes=[
            pltpu.VMEM((BLK, KV), BF16),
            pltpu.VMEM((8 * TOK, BLK), BF16),
            pltpu.VMEM((8 * TOK, KV), BF16),
            pltpu.VMEM((256, KV), BF16),
            pltpu.VMEM((8 * TOK, BLK), BF16),
            pltpu.VMEM((8 * TOK, BLK), BF16),
            pltpu.VMEM((2, 8, SH, KV), F32),
            pltpu.VMEM((2, 8, SH, KV), F32),
            pltpu.VMEM((2, 8, SH, KV), F32),
            pltpu.VMEM((2, 4, 2, SH, KV), BF16),
            pltpu.VMEM((2, 4, 2, SH, KV), BF16),
            pltpu.VMEM((SH, KV), F32),
            pltpu.VMEM((SH, KV), F32),
            pltpu.VMEM((2, 2, 8, 2, SH, HALF), BF16),
            pltpu.VMEM((4, 2, 256, QUAD), BF16),
            pltpu.VMEM((4, 2, 256, QUAD), BF16),
            pltpu.VMEM((4, 4, TOK, QUAD), BF16),
            pltpu.VMEM((4, 4, TOK, QUAD), BF16),
            pltpu.VMEM((4, 4, TOK, QUAD), F32),
            dma((4,)),
            dma((3,)), dma((3,)),
            dma((3, 4)), dma((3, 4)),
            dma((8, 11)), dma((8, 11)),
            dma((11,)), dma((11,)),
            dma((11,)), dma((11,)),
            dma((4, 2)), dma((4, 2)),
            dma((4, 3)), dma((4, 3)),
            dma((8,)), dma((8,)),
            dma((2, 4, 2)), dma((2, 4, 2)),
            dma, dma,
            dma((2, 2, 4, 2)), dma((2, 2, 4, 2)),
            dma((2,)), dma((2,)),
            dma((2, 2, 8)), dma((2, 2, 8)),
        ],
        compiler_params=pltpu.CompilerParams(collective_id=0, has_side_effects=True, vmem_limit_bytes=60 * 1024 * 1024),
    )(activations, cotangent, inner_weight, outer_weight, outer_momentum, next_activations)
    return ig, nk, no, nm


def solution(mesh):
    in_specs = (
        P(("island", "fsdp"), None),
        P(("island", "fsdp"), None),
        P("island", "fsdp", None),
        P(("fsdp", "island"), None),
        P(("fsdp", "island"), None),
        P(("island", "fsdp"), None),
    )
    out_specs = (
        P(("island", "fsdp"), None),
        P(("island", "fsdp"), None),
        P(("fsdp", "island"), None),
        P(("fsdp", "island"), None),
    )
    return jax.shard_map(local, mesh=mesh, in_specs=in_specs, out_specs=out_specs, check_vma=False)
```

```python
import functools

import jax
import jax.numpy as jnp
from jax import lax
from jax.experimental import pallas as pl
from jax.experimental.pallas import tpu as pltpu
from jax.sharding import PartitionSpec as P

inner_rate = 1.2
outer_rate = 0.7
nesterov = 0.9

TOK = 128
BLK = 1024
KV = 1024
SH = 32
HALF = 512
QUAD = 256
XEARLY = 4
F32 = jnp.float32
BF16 = jnp.bfloat16
MESH = pl.DeviceIdType.MESH


def kernel(x, g, w, ow, om, na, ig, nk, no, nm,
           wv, xr, gr, glo, nar, igs, mine, tosib, fromsib, zs, zr, xs, xrv, nw, ksx, krx, ksy, kry, acc,
           loc, gys, gyr, gxs, gxr, xss, xrs, nss, nrs, iss, irs, kxs, kxr, kys, kyr, bss, brs, zss, zrs, hss, hrs,
           ass_, ars, axs, axr, sss, srs):
    isl = lax.axis_index("island")
    f = lax.axis_index("fsdp")
    core = isl % 2
    z = (isl // 2) % 8
    h = isl // 16
    yy = f // 2
    xl = f % 2
    across = (1 - h) * 16 + z * 2 + core

    def same(dy):
        return {"island": isl, "fsdp": ((yy + dy) % 4) * 2 + xl}

    def low(dy):
        return {"island": isl, "fsdp": ((yy + dy) % 4) * 2 + 1 - xl}

    def high(dy):
        return {"island": across, "fsdp": ((yy + dy) % 4) * 2 + 1 - xl}

    sibling = {"island": h * 16 + z * 2 + 1 - core, "fsdp": f}
    partner = {"island": across, "fsdp": f}
    zdev = [
        {"island": h * 16 + ((z + 1) % 8) * 2 + core, "fsdp": f},
        {"island": h * 16 + ((z + 7) % 8) * 2 + core, "fsdp": f},
    ]
    routes = [(same(dy), 0, TOK, yy * TOK) for dy in (1, 3, 2)]
    routes += [(low(dy), 0, 64, 512 + yy * 64) for dy in range(4)]
    routes += [(high(dy), 64, 64, 768 + yy * 64) for dy in range(4)]

    def at_rows(start, size, step):
        return pl.ds(pl.multiple_of(start, step), size)

    def cols(p):
        return at_rows(p * BLK, BLK, BLK)

    def rcopy(src, dst, ss, rs, dev):
        return pltpu.make_async_remote_copy(src_ref=src, dst_ref=dst, send_sem=ss, recv_sem=rs, device_id=dev, device_id_type=MESH)

    w_load = pltpu.make_async_copy(w.at[0], wv, loc.at[0])
    own = [pltpu.make_async_copy(x.at[:, cols(f)], xr.at[at_rows(yy * TOK, TOK, TOK)], loc.at[1]),
           pltpu.make_async_copy(na.at[:, cols(f)], nar.at[at_rows(yy * TOK, TOK, TOK)], loc.at[2])]
    w_load.start()
    own[0].start()
    own[1].start()

    barrier = pltpu.get_barrier_semaphore()
    for dev in [r[0] for r in routes] + [sibling, partner, zdev[0], zdev[1]]:
        pl.semaphore_signal(barrier, inc=1, device_id=dev, device_id_type=MESH)
    pl.semaphore_wait(barrier, 15)

    def gy_copy(n):
        return rcopy(g, gr.at[at_rows(yy * TOK, TOK, TOK)], gys.at[n], gyr.at[n], routes[n][0])

    def gx_copy(n, y):
        src = gr.at[at_rows(y * TOK + (0 if n == 0 else 64), 64, 64)]
        if n == 2:
            dst = glo.at[at_rows(y * 64, 64, 64)]
        else:
            dst = gr.at[at_rows(512 + n * 256 + y * 64, 64, 64)]
        return rcopy(src, dst, gxs.at[n, y], gxr.at[n, y], high(0) if n == 1 else low(0))

    def block_place(b):
        group = b // 2
        return (1 - h + b) % 2, (z // 2 + (2 + group * 3 + (group // 2) * 3 + (group // 3) * 2)) % 4

    def x_copy(b, n):
        bh, bz = block_place(b)
        if n >= 7:
            bh = 1 - bh
        row = bh * 512 + bz * 128
        dev, first, size, to = routes[n]
        src = x.at[pl.ds(first, size), at_rows(dev["fsdp"] * BLK + row, 128, 128)]
        return rcopy(src, xr.at[at_rows(to, size, size), at_rows(row, 128, 128)], xss.at[b, n], xrs.at[b, n], dev)

    def na_copy(n):
        dev, first, size, to = routes[n]
        return rcopy(na.at[pl.ds(first, size), cols(dev["fsdp"])], nar.at[at_rows(to, size, size)], nss.at[n], nrs.at[n], dev)

    def ig_copy(n):
        if n < 3:
            dy = (1, 3, 2)[n]
            src, rows, dev = igs.at[at_rows(((yy + dy) % 4) * TOK, TOK, TOK)], pl.ds(0, TOK), same(dy)
        else:
            dy, half = (n - 3) % 4, (n - 3) // 4
            src, rows, dev = igs.at[at_rows(512 + half * 256 + ((yy + dy) % 4) * 64, 64, 64)], pl.ds(half * 64, 64), low(dy)
        return rcopy(src, ig.at[rows, cols(f)], iss.at[n], irs.at[n], dev)

    def send_x(routed):
        def body(b, c):
            for n in routed:
                x_copy(b, n).start()
            return c

        return body

    for n in range(3):
        gy_copy(n).start()
    gr[at_rows(yy * TOK, TOK, TOK)] = g[...]
    for n in range(2):
        rcopy(g.at[pl.ds(n * 64, 64)], gr.at[at_rows(512 + n * 256 + yy * 64, 64, 64)], gxs.at[n, yy], gxr.at[n, yy],
              high(0) if n == 1 else low(0)).start()
    lax.fori_loop(0, XEARLY, send_x(range(3)), 0)
    for n, dy in enumerate((1, 3, 2)):
        gy_copy(n).wait_recv()
        for m in range(2):
            gx_copy(m, (yy + 4 - dy) % 4).start()
    lax.fori_loop(0, XEARLY, send_x(range(3, 11)), 0)
    lax.fori_loop(XEARLY, 8, send_x(range(11)), 0)
    rcopy(g.at[pl.ds(64, 64)], glo.at[at_rows(yy * 64, 64, 64)], gxs.at[2, yy], gxr.at[2, yy], low(0)).start()
    for dy in (1, 3, 2):
        gx_copy(2, (yy + 4 - dy) % 4).start()

    w_load.wait()

    def grad_cols(values):
        return lax.dot_general(values, wv[...], (((1,), (1,)), ((), ())), preferred_element_type=F32).astype(BF16)

    def grad_step(k, c):
        rows = at_rows(k * TOK, TOK, TOK)
        igs[rows] = grad_cols(gr[rows])
        return c

    lax.fori_loop(0, 4, grad_step, 0)
    for m in range(2):
        for y in range(4):
            gx_copy(m, y).wait_recv()
    lax.fori_loop(4, 6, grad_step, 0)
    for n in range(3):
        na_copy(n).start()
    for n in range(3, 7):
        ig_copy(n).start()
    for n in range(3):
        ig_copy(n).start()

    own[0].wait()

    def sib_copy(b):
        bh, bz = block_place(b)
        return rcopy(tosib.at[bh, pl.ds(bz * 2, 2)], fromsib.at[bh, pl.ds(bz * 2, 2)], bss.at[b], brs.at[b], sibling)

    def block_step(b, c):
        for n in range(11):
            x_copy(b, n).wait_recv()
        bh, bz = block_place(b)
        row = at_rows(bh * 512 + bz * 128, 128, 128)
        grad = lax.dot_general(xr[:, row], gr[...], (((0,), (0,)), ((), ())), preferred_element_type=F32)
        new = wv[row].astype(F32) - inner_rate * (grad * (1.0 / 1024))
        new = new.reshape(2, 2, SH, KV)

        @pl.when(core == 0)
        def _():
            mine[bh, pl.ds(bz * 2, 2)] = new[:, 0]
            tosib[bh, pl.ds(bz * 2, 2)] = new[:, 1]

        @pl.when(core == 1)
        def _():
            mine[bh, pl.ds(bz * 2, 2)] = new[:, 1]
            tosib[bh, pl.ds(bz * 2, 2)] = new[:, 0]

        sib_copy(b).start()
        return c

    def z_copy(dirn, s, piece):
        return rcopy(zs.at[dirn, s, piece], zr.at[dirn, s, piece], zss.at[dirn, s, piece], zrs.at[dirn, s, piece], zdev[dirn])

    def used(dirn, s, piece):
        return s > 0 or piece == dirn

    def plane(piece):
        return h if piece else 1 - h

    def ring_step(s, dirns, piece):
        for dirn in dirns:
            if not used(dirn, s, piece):
                continue
            t = (z + (4 - s if dirn == 0 else 4 + s)) % 8
            total = mine[plane(piece), t] + fromsib[plane(piece), t]
            if s > 0 and used(dirn, s - 1, piece):
                z_copy(dirn, s - 1, piece).wait_recv()
                total = total + zr[dirn, s - 1, piece].astype(F32)
            zs[dirn, s, piece] = total.astype(BF16)
            z_copy(dirn, s, piece).start()

    for group in range(4):
        lax.fori_loop(2 * group, 2 * group + 2, block_step, 0)
        s, dirns = ((0, (0, 1)), (1, (0,)), (1, (1,)), (3, (0, 1)))[group]
        for piece in range(2):
            sib_copy(2 * group + piece).wait_recv()
            ring_step(s, dirns, piece)
        if group == 2:
            for piece in range(2):
                ring_step(2, (0, 1), piece)

    def z_total(piece):
        for dirn in range(2):
            z_copy(dirn, 3, piece).wait_recv()
        at = plane(piece)
        return mine[at, z] + fromsib[at, z] + zr[0, 3, piece].astype(F32) + zr[1, 3, piece].astype(F32)

    pair = rcopy(xs, xrv, hss, hrs, partner)
    xs[...] = z_total(0)
    pair.start()
    own_sum = z_total(1)
    pair.wait_recv()
    summed = own_sum + xrv[...]
    pseudo = ow[...] - summed / 32
    momentum = nesterov * om[...] + pseudo
    outer = ow[...] - outer_rate * (pseudo + nesterov * momentum)
    nm[...] = momentum
    no[...] = outer

    share = outer.astype(BF16)
    for part in range(2):
        nw[part, h, z, core] = share[:, part * HALF:(part + 1) * HALF]

    def spread(part, ph, pz, ss, rs, dev):
        at = nw.at[part, ph, pz, core]
        return rcopy(at, at, ss, rs, dev)

    def ring_copy(part, dirn, d, piece):
        pz = (z + (8 - d if dirn == 0 else d)) % 8
        return spread(part, piece, pz, ass_.at[part, dirn, d, piece], ars.at[part, dirn, d, piece], zdev[dirn])

    def ring_first(part, ph):
        for dirn in range(2):
            spread(part, ph, z, ass_.at[part, dirn, 0, ph], ars.at[part, dirn, 0, ph], zdev[dirn]).start()

    def sib_spread(part, ph, pz):
        return spread(part, ph, pz, sss.at[part, ph, pz], srs.at[part, ph, pz], sibling)

    def cross(part):
        return spread(part, h, z, axs.at[part], axr.at[part], partner)

    for part in range(2):
        cross(part).start()
    for part in range(2):
        ring_first(part, h)
        sib_spread(part, h, z).start()
    for n in range(3, 11):
        na_copy(n).start()
    for part in range(2):
        cross(part).wait_recv()
        ring_first(part, 1 - h)
        sib_spread(part, 1 - h, z).start()
    for y in range(4):
        gx_copy(2, y).wait_recv()

    def late_step(k, c):
        igs[at_rows(768 + k * TOK, TOK, TOK)] = grad_cols(glo[at_rows(k * TOK, TOK, TOK)])
        return c

    lax.fori_loop(0, 2, late_step, 0)
    for n in range(7, 11):
        ig_copy(n).start()
    ig_own = pltpu.make_async_copy(igs.at[at_rows(yy * TOK, TOK, TOK)], ig.at[:, cols(f)], loc.at[3])
    ig_own.start()

    def ring_arrival(part, d):
        for piece in range(2):
            for dirn in range(2):
                if d == 3 and piece != dirn:
                    continue
                ring_copy(part, dirn, d, piece).wait_recv()
                if d < (3 if piece == dirn else 2):
                    ring_copy(part, dirn, d + 1, piece).start()
                sib_spread(part, piece, (z + (7 - d if dirn == 0 else d + 1)) % 8).start()

    for d in range(4):
        for part in range(2):
            ring_arrival(part, d)

    def kx_copy(q, side):
        return rcopy(ksx.at[q, side], krx.at[q, side], kxs.at[q, side], kxr.at[q, side], high(0) if side else low(0))

    def ky_copy(q, n):
        dy = (1, 3, 2)[n]
        return rcopy(ksy.at[q, (yy + dy) % 4], kry.at[q, yy], kys.at[q, n], kyr.at[q, n], same(dy))

    def weight(q):
        return nw[q // 2, :, :, :, :, pl.ds(q % 2 * QUAD, QUAD)].reshape(BLK, QUAD)

    own[1].wait()
    for n in range(11):
        na_copy(n).wait_recv()
    for q in range(4):
        if q % 2 == 0:
            for ph in range(2):
                for pz in range(8):
                    sib_spread(q // 2, ph, pz).wait_recv()
        for side in range(2):
            ksx[q, side] = jnp.dot(nar[pl.ds(512 + side * 256, 256)], weight(q), preferred_element_type=F32).astype(BF16)
            kx_copy(q, side).start()
    for q in range(4):
        acc[q] = jnp.dot(nar[pl.ds(0, 512)], weight(q), preferred_element_type=F32).reshape(4, TOK, QUAD)
    for q in range(4):
        for side in range(2):
            kx_copy(q, side).wait_recv()

        def pair_sum(y):
            other = jnp.concatenate([krx[q, 0, at_rows(y * 64, 64, 64)], krx[q, 1, at_rows(y * 64, 64, 64)]], axis=0)
            return acc[q, y] + other.astype(F32)

        for n in range(3):
            to = (yy + (1, 3, 2)[n]) % 4
            ksy[q, to] = pair_sum(to).astype(BF16)
            ky_copy(q, n).start()
        acc[q, yy] = pair_sum(yy)
    for q in range(4):
        total = acc[q, yy]
        for n in range(3):
            ky_copy(q, n).wait_recv()
            total = total + kry[q, (yy + 4 - (1, 3, 2)[n]) % 4].astype(F32)
        nk[:, pl.ds(q * QUAD, QUAD)] = total.astype(BF16)

    for n in range(11):
        ig_copy(n).wait_recv()
    ig_own.wait()
    for n in range(11):
        ig_copy(n).wait_send()
        na_copy(n).wait_send()
    for n in range(3):
        gy_copy(n).wait_send()
        for y in range(4):
            gx_copy(n, y).wait_send()

    def drain_x(b, c):
        for n in range(11):
            x_copy(b, n).wait_send()
        return c

    lax.fori_loop(0, 8, drain_x, 0)
    for b in range(8):
        sib_copy(b).wait_send()
    for s in range(4):
        for piece in range(2):
            for dirn in range(2):
                if used(dirn, s, piece):
                    z_copy(dirn, s, piece).wait_send()
    pair.wait_send()
    for part in range(2):
        cross(part).wait_send()
        for d in range(4):
            for piece in range(2):
                for dirn in range(2):
                    if d < 3 or piece == dirn:
                        ring_copy(part, dirn, d, piece).wait_send()
        for ph in range(2):
            for pz in range(8):
                sib_spread(part, ph, pz).wait_send()
    for q in range(4):
        for side in range(2):
            kx_copy(q, side).wait_send()
        for n in range(3):
            ky_copy(q, n).wait_send()


def move(*refs):
    sources, targets, (wide, keys, outer, momentum, got, put) = refs[:4], refs[4:8], refs[8:]
    steps = []
    for n in range(8):
        at = (slice(None), pl.ds(n * BLK, BLK))
        steps.append((sources[0].at[at], wide.at[at], targets[0].at[at]))
    for source, between, target in zip(sources[1:], (keys, outer, momentum), targets[1:]):
        steps.append((source, between, target))
    into = [pltpu.make_async_copy(a, b, got.at[n]) for n, (a, b, _) in enumerate(steps)]
    out = [pltpu.make_async_copy(b, c, put.at[n]) for n, (_, b, c) in enumerate(steps)]
    for copy in into:
        copy.start()
    for n, copy in enumerate(into):
        copy.wait()
        out[n].start()
    for copy in out:
        copy.wait()


def hand_over(arrays):
    hb = pl.BlockSpec(memory_space=pl.ANY)
    return pl.pallas_call(
        move,
        out_shape=tuple(jax.ShapeDtypeStruct(a.shape, a.dtype) for a in arrays),
        in_specs=[hb] * 4,
        out_specs=(hb,) * 4,
        scratch_shapes=[pltpu.VMEM(a.shape, a.dtype) for a in arrays]
        + [pltpu.SemaphoreType.DMA((11,)), pltpu.SemaphoreType.DMA((11,))],
    )(*arrays)


def local(activations, cotangent, inner_weight, outer_weight, outer_momentum, next_activations):
    vm = pl.BlockSpec(memory_space=pltpu.VMEM)
    hb = pl.BlockSpec(memory_space=pl.ANY)
    dma = pltpu.SemaphoreType.DMA
    ig, nk, no, nm = pl.pallas_call(
        kernel,
        out_shape=(
            jax.ShapeDtypeStruct((TOK, 8 * BLK), BF16),
            jax.ShapeDtypeStruct((TOK, KV), BF16),
            jax.ShapeDtypeStruct((SH, KV), F32),
            jax.ShapeDtypeStruct((SH, KV), F32),
        ),
        in_specs=[hb, vm, hb, vm, vm, hb],
        out_specs=(hb, vm, vm, vm),
        scratch_shapes=[
            pltpu.VMEM((BLK, KV), BF16),
            pltpu.VMEM((8 * TOK, BLK), BF16),
            pltpu.VMEM((8 * TOK, KV), BF16),
            pltpu.VMEM((256, KV), BF16),
            pltpu.VMEM((8 * TOK, BLK), BF16),
            pltpu.VMEM((8 * TOK, BLK), BF16),
            pltpu.VMEM((2, 8, SH, KV), F32),
            pltpu.VMEM((2, 8, SH, KV), F32),
            pltpu.VMEM((2, 8, SH, KV), F32),
            pltpu.VMEM((2, 4, 2, SH, KV), BF16),
            pltpu.VMEM((2, 4, 2, SH, KV), BF16),
            pltpu.VMEM((SH, KV), F32),
            pltpu.VMEM((SH, KV), F32),
            pltpu.VMEM((2, 2, 8, 2, SH, HALF), BF16),
            pltpu.VMEM((4, 2, 256, QUAD), BF16),
            pltpu.VMEM((4, 2, 256, QUAD), BF16),
            pltpu.VMEM((4, 4, TOK, QUAD), BF16),
            pltpu.VMEM((4, 4, TOK, QUAD), BF16),
            pltpu.VMEM((4, 4, TOK, QUAD), F32),
            dma((4,)),
            dma((3,)), dma((3,)),
            dma((3, 4)), dma((3, 4)),
            dma((8, 11)), dma((8, 11)),
            dma((11,)), dma((11,)),
            dma((11,)), dma((11,)),
            dma((4, 2)), dma((4, 2)),
            dma((4, 3)), dma((4, 3)),
            dma((8,)), dma((8,)),
            dma((2, 4, 2)), dma((2, 4, 2)),
            dma, dma,
            dma((2, 2, 4, 2)), dma((2, 2, 4, 2)),
            dma((2,)), dma((2,)),
            dma((2, 2, 8)), dma((2, 2, 8)),
        ],
        compiler_params=pltpu.CompilerParams(collective_id=0, has_side_effects=True, vmem_limit_bytes=60 * 1024 * 1024),
    )(activations, cotangent, inner_weight, outer_weight, outer_momentum, next_activations)
    return hand_over((ig, nk, no, nm))


def solution(mesh):
    in_specs = (
        P(("island", "fsdp"), None),
        P(("island", "fsdp"), None),
        P("island", "fsdp", None),
        P(("fsdp", "island"), None),
        P(("fsdp", "island"), None),
        P(("island", "fsdp"), None),
    )
    out_specs = (
        P(("island", "fsdp"), None),
        P(("island", "fsdp"), None),
        P(("fsdp", "island"), None),
        P(("fsdp", "island"), None),
    )
    return jax.shard_map(local, mesh=mesh, in_specs=in_specs, out_specs=out_specs, check_vma=False)
```

```python
import functools

import jax
import jax.numpy as jnp
from jax import lax
from jax.experimental import pallas as pl
from jax.experimental.pallas import tpu as pltpu
from jax.sharding import PartitionSpec as P

inner_rate = 1.2
outer_rate = 0.7
nesterov = 0.9

TOK = 128
BLK = 1024
KV = 1024
SH = 32
HALF = 512
QUAD = 256
XEARLY = 2
XMID = 2
F32 = jnp.float32
BF16 = jnp.bfloat16
MESH = pl.DeviceIdType.MESH


def kernel(x, g, w, ow, om, na, ig, nk, no, nm,
           wv, xr, gr, glo, nar, igs, mine, tosib, fromsib, zs, zr, xs, xrv, nw, ksx, krx, ksy, kry, acc,
           loc, gys, gyr, gxs, gxr, xss, xrs, nss, nrs, iss, irs, kxs, kxr, kys, kyr, bss, brs, zss, zrs, hss, hrs,
           ass_, ars, axs, axr, sss, srs):
    isl = lax.axis_index("island")
    f = lax.axis_index("fsdp")
    core = isl % 2
    z = (isl // 2) % 8
    h = isl // 16
    yy = f // 2
    xl = f % 2
    across = (1 - h) * 16 + z * 2 + core

    def same(dy):
        return {"island": isl, "fsdp": ((yy + dy) % 4) * 2 + xl}

    def low(dy):
        return {"island": isl, "fsdp": ((yy + dy) % 4) * 2 + 1 - xl}

    def high(dy):
        return {"island": across, "fsdp": ((yy + dy) % 4) * 2 + 1 - xl}

    sibling = {"island": h * 16 + z * 2 + 1 - core, "fsdp": f}
    partner = {"island": across, "fsdp": f}
    zdev = [
        {"island": h * 16 + ((z + 1) % 8) * 2 + core, "fsdp": f},
        {"island": h * 16 + ((z + 7) % 8) * 2 + core, "fsdp": f},
    ]
    routes = [(same(dy), 0, TOK, yy * TOK) for dy in (1, 3, 2)]
    for dy in range(4):
        routes += [(low(dy), 0, 64, 512 + yy * 64), (high(dy), 64, 64, 768 + yy * 64)]

    def at_rows(start, size, step):
        return pl.ds(pl.multiple_of(start, step), size)

    def cols(p):
        return at_rows(p * BLK, BLK, BLK)

    def rcopy(src, dst, ss, rs, dev):
        return pltpu.make_async_remote_copy(src_ref=src, dst_ref=dst, send_sem=ss, recv_sem=rs, device_id=dev, device_id_type=MESH)

    w_load = pltpu.make_async_copy(w.at[0], wv, loc.at[0])
    own = [pltpu.make_async_copy(x.at[:, cols(f)], xr.at[at_rows(yy * TOK, TOK, TOK)], loc.at[1]),
           pltpu.make_async_copy(na.at[:, cols(f)], nar.at[at_rows(yy * TOK, TOK, TOK)], loc.at[2])]
    g_own = pltpu.make_async_copy(g, gr.at[at_rows(yy * TOK, TOK, TOK)], loc.at[2 + 2])
    w_load.start()
    g_own.start()
    own[0].start()
    own[1].start()

    barrier = pltpu.get_barrier_semaphore()
    for dev in [r[0] for r in routes] + [sibling, partner, zdev[0], zdev[1]]:
        pl.semaphore_signal(barrier, inc=1, device_id=dev, device_id_type=MESH)
    pl.semaphore_wait(barrier, 15)

    def gy_copy(n):
        return rcopy(g, gr.at[at_rows(yy * TOK, TOK, TOK)], gys.at[n], gyr.at[n], routes[n][0])

    def gz_copy(n):
        rows = at_rows(((yy + (3, 1)[n]) % 4) * TOK + n * 64, 64, 64)
        return rcopy(gr.at[rows], gr.at[rows], gys.at[2 + n], gyr.at[2 + n], routes[n][0])

    def gx_copy(n, y):
        src = gr.at[at_rows(y * TOK + (0 if n == 0 else 64), 64, 64)]
        if n == 2:
            dst = glo.at[at_rows(y * 64, 64, 64)]
        else:
            dst = gr.at[at_rows(512 + n * 256 + y * 64, 64, 64)]
        return rcopy(src, dst, gxs.at[n, y], gxr.at[n, y], high(0) if n == 1 else low(0))

    def block_place(b):
        group = b // 2
        return (1 - h + b) % 2, (z // 2 + (2 + group * 3 + (group // 2) * 3 + (group // 3) * 2)) % 4

    def x_copy(b, n):
        bh, bz = block_place(b)
        if n >= 3 and n % 2 == 0:
            bh = 1 - bh
        row = bh * 512 + bz * 128
        dev, first, size, to = routes[n]
        src = x.at[pl.ds(first, size), at_rows(dev["fsdp"] * BLK + row, 128, 128)]
        return rcopy(src, xr.at[at_rows(to, size, size), at_rows(row, 128, 128)], xss.at[b, n], xrs.at[b, n], dev)

    def na_copy(n):
        dev, first, size, to = routes[n]
        return rcopy(na.at[pl.ds(first, size), cols(dev["fsdp"])], nar.at[at_rows(to, size, size)], nss.at[n], nrs.at[n], dev)

    def ig_copy(n):
        if n < 3:
            dy = (1, 3, 2)[n]
            src, rows, dev = igs.at[at_rows(((yy + dy) % 4) * TOK, TOK, TOK)], pl.ds(0, TOK), same(dy)
        else:
            dy, half = (n - 3) % 4, (n - 3) // 4
            src, rows, dev = igs.at[at_rows(512 + half * 256 + ((yy + dy) % 4) * 64, 64, 64)], pl.ds(half * 64, 64), low(dy)
        return rcopy(src, ig.at[rows, cols(f)], iss.at[n], irs.at[n], dev)

    def send_x(routed):
        def body(b, c):
            for n in routed:
                x_copy(b, n).start()
            return c

        return body

    for n in range(2):
        gy_copy(n).start()
    g_own.wait()
    for n in range(2):
        rcopy(g.at[pl.ds(n * 64, 64)], gr.at[at_rows(512 + n * 256 + yy * 64, 64, 64)], gxs.at[n, yy], gxr.at[n, yy],
              high(0) if n == 1 else low(0)).start()
    lax.fori_loop(0, XEARLY, send_x(range(3)), 0)
    for n, dy in enumerate((1, 3)):
        gy_copy(n).wait_recv()
        gz_copy(n).start()
        for m in range(2):
            gx_copy(m, (yy + 4 - dy) % 4).start()
    lax.fori_loop(0, XEARLY, send_x(range(3, 11)), 0)
    lax.fori_loop(XEARLY, XMID, send_x(range(11)), 0)
    for n in range(2):
        gz_copy(n).wait_recv()
        gx_copy(n, (yy + 2) % 4).start()
    lax.fori_loop(XMID, 8, send_x(range(11)), 0)
    rcopy(g.at[pl.ds(64, 64)], glo.at[at_rows(yy * 64, 64, 64)], gxs.at[2, yy], gxr.at[2, yy], low(0)).start()
    for dy in (1, 3, 2):
        gx_copy(2, (yy + 4 - dy) % 4).start()

    w_load.wait()

    def grad_cols(values):
        return lax.dot_general(values, wv[...], (((1,), (1,)), ((), ())), preferred_element_type=F32).astype(BF16)

    def grad_step(k, c):
        rows = at_rows(k * TOK, TOK, TOK)
        igs[rows] = grad_cols(gr[rows])
        return c

    lax.fori_loop(0, 4, grad_step, 0)
    for m in range(2):
        for y in range(4):
            gx_copy(m, y).wait_recv()
    lax.fori_loop(4, 6, grad_step, 0)
    for n in range(3):
        na_copy(n).start()
    for n in range(3, 7):
        ig_copy(n).start()
    for n in range(3):
        ig_copy(n).start()

    own[0].wait()

    def sib_copy(b):
        bh, bz = block_place(b)
        return rcopy(tosib.at[bh, pl.ds(bz * 2, 2)], fromsib.at[bh, pl.ds(bz * 2, 2)], bss.at[b], brs.at[b], sibling)

    def block_step(b, c):
        for n in range(11):
            x_copy(b, n).wait_recv()
        bh, bz = block_place(b)
        row = at_rows(bh * 512 + bz * 128, 128, 128)
        grad = lax.dot_general(xr[:, row], gr[...], (((0,), (0,)), ((), ())), preferred_element_type=F32)
        new = wv[row].astype(F32) - inner_rate * (grad * (1.0 / 1024))
        new = new.reshape(2, 2, SH, KV)

        @pl.when(core == 0)
        def _():
            mine[bh, pl.ds(bz * 2, 2)] = new[:, 0]
            tosib[bh, pl.ds(bz * 2, 2)] = new[:, 1]

        @pl.when(core == 1)
        def _():
            mine[bh, pl.ds(bz * 2, 2)] = new[:, 1]
            tosib[bh, pl.ds(bz * 2, 2)] = new[:, 0]

        sib_copy(b).start()
        return c

    def z_copy(dirn, s, piece):
        return rcopy(zs.at[dirn, s, piece], zr.at[dirn, s, piece], zss.at[dirn, s, piece], zrs.at[dirn, s, piece], zdev[dirn])

    def used(dirn, s, piece):
        return s > 0 or piece == dirn

    def plane(piece):
        return h if piece else 1 - h

    def ring_step(s, dirns, piece):
        for dirn in dirns:
            if not used(dirn, s, piece):
                continue
            t = (z + (4 - s if dirn == 0 else 4 + s)) % 8
            total = mine[plane(piece), t] + fromsib[plane(piece), t]
            if s > 0 and used(dirn, s - 1, piece):
                z_copy(dirn, s - 1, piece).wait_recv()
                total = total + zr[dirn, s - 1, piece].astype(F32)
            zs[dirn, s, piece] = total.astype(BF16)
            z_copy(dirn, s, piece).start()

    for group in range(4):
        lax.fori_loop(2 * group, 2 * group + 2, block_step, 0)
        s, dirns = ((0, (0, 1)), (1, (0,)), (1, (1,)), (3, (0, 1)))[group]
        for piece in range(2):
            sib_copy(2 * group + piece).wait_recv()
            ring_step(s, dirns, piece)
        if group == 2:
            for piece in range(2):
                ring_step(2, (0, 1), piece)

    def z_total(piece):
        for dirn in range(2):
            z_copy(dirn, 3, piece).wait_recv()
        at = plane(piece)
        return mine[at, z] + fromsib[at, z] + zr[0, 3, piece].astype(F32) + zr[1, 3, piece].astype(F32)

    pair = rcopy(xs, xrv, hss, hrs, partner)
    xs[...] = z_total(0)
    pair.start()
    own_sum = z_total(1)
    pair.wait_recv()
    summed = own_sum + xrv[...]
    pseudo = ow[...] - summed / 32
    momentum = nesterov * om[...] + pseudo
    outer = ow[...] - outer_rate * (pseudo + nesterov * momentum)
    nm[...] = momentum
    no[...] = outer

    share = outer.astype(BF16)
    for part in range(2):
        nw[part, h, z, core] = share[:, part * HALF:(part + 1) * HALF]

    def spread(part, ph, pz, ss, rs, dev):
        at = nw.at[part, ph, pz, core]
        return rcopy(at, at, ss, rs, dev)

    def ring_copy(part, dirn, d, piece):
        pz = (z + (8 - d if dirn == 0 else d)) % 8
        return spread(part, piece, pz, ass_.at[part, dirn, d, piece], ars.at[part, dirn, d, piece], zdev[dirn])

    def ring_first(part, ph):
        for dirn in range(2):
            spread(part, ph, z, ass_.at[part, dirn, 0, ph], ars.at[part, dirn, 0, ph], zdev[dirn]).start()

    def sib_spread(part, ph, pz):
        return spread(part, ph, pz, sss.at[part, ph, pz], srs.at[part, ph, pz], sibling)

    def cross(part):
        return spread(part, h, z, axs.at[part], axr.at[part], partner)

    for part in range(2):
        cross(part).start()
    for part in range(2):
        ring_first(part, h)
        sib_spread(part, h, z).start()
    for n in range(3, 11):
        na_copy(n).start()
    for part in range(2):
        cross(part).wait_recv()
        ring_first(part, 1 - h)
        sib_spread(part, 1 - h, z).start()
    for y in range(4):
        gx_copy(2, y).wait_recv()

    def late_step(k, c):
        igs[at_rows(768 + k * TOK, TOK, TOK)] = grad_cols(glo[at_rows(k * TOK, TOK, TOK)])
        return c

    lax.fori_loop(0, 2, late_step, 0)
    for n in range(7, 11):
        ig_copy(n).start()
    ig_own = pltpu.make_async_copy(igs.at[at_rows(yy * TOK, TOK, TOK)], ig.at[:, cols(f)], loc.at[3])
    ig_own.start()

    def ring_arrival(part, d):
        for piece in range(2):
            for dirn in range(2):
                if d == 3 and piece != dirn:
                    continue
                ring_copy(part, dirn, d, piece).wait_recv()
                if d < (3 if piece == dirn else 2):
                    ring_copy(part, dirn, d + 1, piece).start()
                sib_spread(part, piece, (z + (7 - d if dirn == 0 else d + 1)) % 8).start()

    for d in range(4):
        for part in range(2):
            ring_arrival(part, d)

    def kx_copy(q, side):
        return rcopy(ksx.at[q, side], krx.at[q, side], kxs.at[q, side], kxr.at[q, side], high(0) if side else low(0))

    def ky_copy(q, n):
        dy = (1, 3, 2)[n]
        return rcopy(ksy.at[q, (yy + dy) % 4], kry.at[q, yy], kys.at[q, n], kyr.at[q, n], same(dy))

    def weight(q):
        return nw[q // 2, :, :, :, :, pl.ds(q % 2 * QUAD, QUAD)].reshape(BLK, QUAD)

    own[1].wait()
    for n in range(11):
        na_copy(n).wait_recv()
    for q in range(4):
        if q % 2 == 0:
            for ph in range(2):
                for pz in range(8):
                    sib_spread(q // 2, ph, pz).wait_recv()
        for side in range(2):
            ksx[q, side] = jnp.dot(nar[pl.ds(512 + side * 256, 256)], weight(q), preferred_element_type=F32).astype(BF16)
            kx_copy(q, side).start()
    for q in range(4):
        acc[q] = jnp.dot(nar[pl.ds(0, 512)], weight(q), preferred_element_type=F32).reshape(4, TOK, QUAD)
    for q in range(4):
        for side in range(2):
            kx_copy(q, side).wait_recv()

        def pair_sum(y):
            other = jnp.concatenate([krx[q, 0, at_rows(y * 64, 64, 64)], krx[q, 1, at_rows(y * 64, 64, 64)]], axis=0)
            return acc[q, y] + other.astype(F32)

        for n in range(3):
            to = (yy + (1, 3, 2)[n]) % 4
            ksy[q, to] = pair_sum(to).astype(BF16)
            ky_copy(q, n).start()
        acc[q, yy] = pair_sum(yy)
    for q in range(4):
        total = acc[q, yy]
        for n in range(3):
            ky_copy(q, n).wait_recv()
            total = total + kry[q, (yy + 4 - (1, 3, 2)[n]) % 4].astype(F32)
        nk[:, pl.ds(q * QUAD, QUAD)] = total.astype(BF16)

    for n in range(11):
        ig_copy(n).wait_recv()
    ig_own.wait()
    for n in range(11):
        ig_copy(n).wait_send()
        na_copy(n).wait_send()
    for n in range(2):
        gy_copy(n).wait_send()
        gz_copy(n).wait_send()
    for n in range(3):
        for y in range(4):
            gx_copy(n, y).wait_send()

    def drain_x(b, c):
        for n in range(11):
            x_copy(b, n).wait_send()
        return c

    lax.fori_loop(0, 8, drain_x, 0)
    for b in range(8):
        sib_copy(b).wait_send()
    for s in range(4):
        for piece in range(2):
            for dirn in range(2):
                if used(dirn, s, piece):
                    z_copy(dirn, s, piece).wait_send()
    pair.wait_send()
    for part in range(2):
        cross(part).wait_send()
        for d in range(4):
            for piece in range(2):
                for dirn in range(2):
                    if d < 3 or piece == dirn:
                        ring_copy(part, dirn, d, piece).wait_send()
        for ph in range(2):
            for pz in range(8):
                sib_spread(part, ph, pz).wait_send()
    for q in range(4):
        for side in range(2):
            kx_copy(q, side).wait_send()
        for n in range(3):
            ky_copy(q, n).wait_send()


def move(*refs):
    sources, targets, (wide, keys, outer, momentum, got, put) = refs[:4], refs[4:8], refs[8:]
    steps = []
    for n in range(8):
        at = (slice(None), pl.ds(n * BLK, BLK))
        steps.append((sources[0].at[at], wide.at[at], targets[0].at[at]))
    for source, between, target in zip(sources[1:], (keys, outer, momentum), targets[1:]):
        steps.append((source, between, target))
    into = [pltpu.make_async_copy(a, b, got.at[n]) for n, (a, b, _) in enumerate(steps)]
    out = [pltpu.make_async_copy(b, c, put.at[n]) for n, (_, b, c) in enumerate(steps)]
    for copy in into:
        copy.start()
    for n, copy in enumerate(into):
        copy.wait()
        out[n].start()
    for copy in out:
        copy.wait()


def hand_over(arrays):
    hb = pl.BlockSpec(memory_space=pl.ANY)
    return pl.pallas_call(
        move,
        out_shape=tuple(jax.ShapeDtypeStruct(a.shape, a.dtype) for a in arrays),
        in_specs=[hb] * 4,
        out_specs=(hb,) * 4,
        scratch_shapes=[pltpu.VMEM(a.shape, a.dtype) for a in arrays]
        + [pltpu.SemaphoreType.DMA((11,)), pltpu.SemaphoreType.DMA((11,))],
    )(*arrays)


def local(activations, cotangent, inner_weight, outer_weight, outer_momentum, next_activations):
    vm = pl.BlockSpec(memory_space=pltpu.VMEM)
    hb = pl.BlockSpec(memory_space=pl.ANY)
    dma = pltpu.SemaphoreType.DMA
    ig, nk, no, nm = pl.pallas_call(
        kernel,
        out_shape=(
            jax.ShapeDtypeStruct((TOK, 8 * BLK), BF16),
            jax.ShapeDtypeStruct((TOK, KV), BF16),
            jax.ShapeDtypeStruct((SH, KV), F32),
            jax.ShapeDtypeStruct((SH, KV), F32),
        ),
        in_specs=[hb, hb, hb, vm, vm, hb],
        out_specs=(hb, vm, vm, vm),
        scratch_shapes=[
            pltpu.VMEM((BLK, KV), BF16),
            pltpu.VMEM((8 * TOK, BLK), BF16),
            pltpu.VMEM((8 * TOK, KV), BF16),
            pltpu.VMEM((256, KV), BF16),
            pltpu.VMEM((8 * TOK, BLK), BF16),
            pltpu.VMEM((8 * TOK, BLK), BF16),
            pltpu.VMEM((2, 8, SH, KV), F32),
            pltpu.VMEM((2, 8, SH, KV), F32),
            pltpu.VMEM((2, 8, SH, KV), F32),
            pltpu.VMEM((2, 4, 2, SH, KV), BF16),
            pltpu.VMEM((2, 4, 2, SH, KV), BF16),
            pltpu.VMEM((SH, KV), F32),
            pltpu.VMEM((SH, KV), F32),
            pltpu.VMEM((2, 2, 8, 2, SH, HALF), BF16),
            pltpu.VMEM((4, 2, 256, QUAD), BF16),
            pltpu.VMEM((4, 2, 256, QUAD), BF16),
            pltpu.VMEM((4, 4, TOK, QUAD), BF16),
            pltpu.VMEM((4, 4, TOK, QUAD), BF16),
            pltpu.VMEM((4, 4, TOK, QUAD), F32),
            dma((5,)),
            dma((4,)), dma((4,)),
            dma((3, 4)), dma((3, 4)),
            dma((8, 11)), dma((8, 11)),
            dma((11,)), dma((11,)),
            dma((11,)), dma((11,)),
            dma((4, 2)), dma((4, 2)),
            dma((4, 3)), dma((4, 3)),
            dma((8,)), dma((8,)),
            dma((2, 4, 2)), dma((2, 4, 2)),
            dma, dma,
            dma((2, 2, 4, 2)), dma((2, 2, 4, 2)),
            dma((2,)), dma((2,)),
            dma((2, 2, 8)), dma((2, 2, 8)),
        ],
        compiler_params=pltpu.CompilerParams(collective_id=0, has_side_effects=True, vmem_limit_bytes=60 * 1024 * 1024),
    )(activations, cotangent, inner_weight, outer_weight, outer_momentum, next_activations)
    return hand_over((ig, nk, no, nm))


def solution(mesh):
    in_specs = (
        P(("island", "fsdp"), None),
        P(("island", "fsdp"), None),
        P("island", "fsdp", None),
        P(("fsdp", "island"), None),
        P(("fsdp", "island"), None),
        P(("island", "fsdp"), None),
    )
    out_specs = (
        P(("island", "fsdp"), None),
        P(("island", "fsdp"), None),
        P(("fsdp", "island"), None),
        P(("fsdp", "island"), None),
    )
    return jax.shard_map(local, mesh=mesh, in_specs=in_specs, out_specs=out_specs, check_vma=False)
```

```python
import functools

import jax
import jax.numpy as jnp
from jax import lax
from jax.experimental import pallas as pl
from jax.experimental.pallas import tpu as pltpu
from jax.sharding import PartitionSpec as P

inner_rate = 1.2
outer_rate = 0.7
nesterov = 0.9

TOK = 128
BLK = 1024
KV = 1024
SH = 32
HALF = 512
QUAD = 256
XEARLY = 3
XMID = 3
F32 = jnp.float32
BF16 = jnp.bfloat16
MESH = pl.DeviceIdType.MESH


def kernel(x, g, w, ow, om, na, ig, nk, no, nm,
           wv, xr, gr, glo, nar, igs, mine, tosib, fromsib, zs, zr, xs, xrv, nw, ksx, krx, ksy, kry, acc,
           loc, gys, gyr, gxs, gxr, xss, xrs, nss, nrs, iss, irs, kxs, kxr, kys, kyr, bss, brs, zss, zrs, hss, hrs,
           ass_, ars, axs, axr, sss, srs):
    isl = lax.axis_index("island")
    f = lax.axis_index("fsdp")
    core = isl % 2
    z = (isl // 2) % 8
    h = isl // 16
    yy = f // 2
    xl = f % 2
    across = (1 - h) * 16 + z * 2 + core

    def same(dy):
        return {"island": isl, "fsdp": ((yy + dy) % 4) * 2 + xl}

    def low(dy):
        return {"island": isl, "fsdp": ((yy + dy) % 4) * 2 + 1 - xl}

    def high(dy):
        return {"island": across, "fsdp": ((yy + dy) % 4) * 2 + 1 - xl}

    sibling = {"island": h * 16 + z * 2 + 1 - core, "fsdp": f}
    partner = {"island": across, "fsdp": f}
    zdev = [
        {"island": h * 16 + ((z + 1) % 8) * 2 + core, "fsdp": f},
        {"island": h * 16 + ((z + 7) % 8) * 2 + core, "fsdp": f},
    ]
    routes = [(same(dy), 0, TOK, yy * TOK) for dy in (1, 3, 2)]
    for dy in range(4):
        routes += [(low(dy), 0, 64, 512 + yy * 64), (high(dy), 64, 64, 768 + yy * 64)]

    def at_rows(start, size, step):
        return pl.ds(pl.multiple_of(start, step), size)

    def cols(p):
        return at_rows(p * BLK, BLK, BLK)

    def rcopy(src, dst, ss, rs, dev):
        return pltpu.make_async_remote_copy(src_ref=src, dst_ref=dst, send_sem=ss, recv_sem=rs, device_id=dev, device_id_type=MESH)

    w_load = pltpu.make_async_copy(w.at[0], wv, loc.at[0])
    own = [pltpu.make_async_copy(x.at[:, cols(f)], xr.at[at_rows(yy * TOK, TOK, TOK)], loc.at[1]),
           pltpu.make_async_copy(na.at[:, cols(f)], nar.at[at_rows(yy * TOK, TOK, TOK)], loc.at[2])]
    g_own = pltpu.make_async_copy(g, gr.at[at_rows(yy * TOK, TOK, TOK)], loc.at[2 + 2])
    w_load.start()
    g_own.start()
    own[0].start()
    own[1].start()

    barrier = pltpu.get_barrier_semaphore()
    for dev in [r[0] for r in routes] + [sibling, partner, zdev[0], zdev[1]]:
        pl.semaphore_signal(barrier, inc=1, device_id=dev, device_id_type=MESH)
    pl.semaphore_wait(barrier, 15)

    def gy_copy(n):
        return rcopy(g, gr.at[at_rows(yy * TOK, TOK, TOK)], gys.at[n], gyr.at[n], routes[n][0])

    def gz_copy(n):
        rows = at_rows(((yy + (3, 1)[n]) % 4) * TOK + n * 64, 64, 64)
        return rcopy(gr.at[rows], gr.at[rows], gys.at[2 + n], gyr.at[2 + n], routes[n][0])

    def gx_copy(n, y):
        src = gr.at[at_rows(y * TOK + (0 if n == 0 else 64), 64, 64)]
        if n == 2:
            dst = glo.at[at_rows(y * 64, 64, 64)]
        else:
            dst = gr.at[at_rows(512 + n * 256 + y * 64, 64, 64)]
        return rcopy(src, dst, gxs.at[n, y], gxr.at[n, y], high(0) if n == 1 else low(0))

    def block_place(b):
        group = b // 2
        return (1 - h + b) % 2, (z // 2 + (2 + group * 3 + (group // 2) * 3 + (group // 3) * 2)) % 4

    def x_copy(b, n):
        bh, bz = block_place(b)
        if n >= 3 and n % 2 == 0:
            bh = 1 - bh
        row = bh * 512 + bz * 128
        dev, first, size, to = routes[n]
        src = x.at[pl.ds(first, size), at_rows(dev["fsdp"] * BLK + row, 128, 128)]
        return rcopy(src, xr.at[at_rows(to, size, size), at_rows(row, 128, 128)], xss.at[b, n], xrs.at[b, n], dev)

    def na_copy(n):
        dev, first, size, to = routes[n]
        return rcopy(na.at[pl.ds(first, size), cols(dev["fsdp"])], nar.at[at_rows(to, size, size)], nss.at[n], nrs.at[n], dev)

    def ig_copy(n):
        if n < 3:
            dy = (1, 3, 2)[n]
            src, rows, dev = igs.at[at_rows(((yy + dy) % 4) * TOK, TOK, TOK)], pl.ds(0, TOK), same(dy)
        else:
            dy, half = (n - 3) % 4, (n - 3) // 4
            src, rows, dev = igs.at[at_rows(512 + half * 256 + ((yy + dy) % 4) * 64, 64, 64)], pl.ds(half * 64, 64), low(dy)
        return rcopy(src, ig.at[rows, cols(f)], iss.at[n], irs.at[n], dev)

    def send_x(routed):
        def body(b, c):
            for n in routed:
                x_copy(b, n).start()
            return c

        return body

    for n in range(2):
        gy_copy(n).start()
    g_own.wait()
    for n in range(2):
        rcopy(g.at[pl.ds(n * 64, 64)], gr.at[at_rows(512 + n * 256 + yy * 64, 64, 64)], gxs.at[n, yy], gxr.at[n, yy],
              high(0) if n == 1 else low(0)).start()
    lax.fori_loop(0, XEARLY, send_x(range(3)), 0)
    for n, dy in enumerate((1, 3)):
        gy_copy(n).wait_recv()
        gz_copy(n).start()
        for m in range(2):
            gx_copy(m, (yy + 4 - dy) % 4).start()
    lax.fori_loop(0, XEARLY, send_x(range(3, 11)), 0)
    lax.fori_loop(XEARLY, XMID, send_x(range(11)), 0)
    for n in range(2):
        gz_copy(n).wait_recv()
        gx_copy(n, (yy + 2) % 4).start()
    lax.fori_loop(XMID, 8, send_x(range(11)), 0)
    rcopy(g.at[pl.ds(64, 64)], glo.at[at_rows(yy * 64, 64, 64)], gxs.at[2, yy], gxr.at[2, yy], low(0)).start()
    for dy in (1, 3, 2):
        gx_copy(2, (yy + 4 - dy) % 4).start()

    w_load.wait()

    def grad_cols(values):
        return lax.dot_general(values, wv[...], (((1,), (1,)), ((), ())), preferred_element_type=F32).astype(BF16)

    def grad_step(k, c):
        rows = at_rows(k * TOK, TOK, TOK)
        igs[rows] = grad_cols(gr[rows])
        return c

    lax.fori_loop(0, 4, grad_step, 0)
    for m in range(2):
        for y in range(4):
            gx_copy(m, y).wait_recv()
    lax.fori_loop(4, 6, grad_step, 0)
    for n in range(3):
        na_copy(n).start()
    for n in range(3, 7):
        ig_copy(n).start()
    for n in range(3):
        ig_copy(n).start()

    own[0].wait()

    def sib_copy(b):
        bh, bz = block_place(b)
        return rcopy(tosib.at[bh, pl.ds(bz * 2, 2)], fromsib.at[bh, pl.ds(bz * 2, 2)], bss.at[b], brs.at[b], sibling)

    def block_step(b, c):
        for n in range(11):
            x_copy(b, n).wait_recv()
        bh, bz = block_place(b)
        row = at_rows(bh * 512 + bz * 128, 128, 128)
        grad = lax.dot_general(xr[:, row], gr[...], (((0,), (0,)), ((), ())), preferred_element_type=F32)
        new = wv[row].astype(F32) - inner_rate * (grad * (1.0 / 1024))
        new = new.reshape(2, 2, SH, KV)

        @pl.when(core == 0)
        def _():
            mine[bh, pl.ds(bz * 2, 2)] = new[:, 0]
            tosib[bh, pl.ds(bz * 2, 2)] = new[:, 1]

        @pl.when(core == 1)
        def _():
            mine[bh, pl.ds(bz * 2, 2)] = new[:, 1]
            tosib[bh, pl.ds(bz * 2, 2)] = new[:, 0]

        sib_copy(b).start()
        return c

    def z_copy(dirn, s, piece):
        return rcopy(zs.at[dirn, s, piece], zr.at[dirn, s, piece], zss.at[dirn, s, piece], zrs.at[dirn, s, piece], zdev[dirn])

    def used(dirn, s, piece):
        return s > 0 or piece == dirn

    def plane(piece):
        return h if piece else 1 - h

    def ring_step(s, dirns, piece):
        for dirn in dirns:
            if not used(dirn, s, piece):
                continue
            t = (z + (4 - s if dirn == 0 else 4 + s)) % 8
            total = mine[plane(piece), t] + fromsib[plane(piece), t]
            if s > 0 and used(dirn, s - 1, piece):
                z_copy(dirn, s - 1, piece).wait_recv()
                total = total + zr[dirn, s - 1, piece].astype(F32)
            zs[dirn, s, piece] = total.astype(BF16)
            z_copy(dirn, s, piece).start()

    for group in range(4):
        lax.fori_loop(2 * group, 2 * group + 2, block_step, 0)
        s, dirns = ((0, (0, 1)), (1, (0,)), (1, (1,)), (3, (0, 1)))[group]
        for piece in range(2):
            sib_copy(2 * group + piece).wait_recv()
            ring_step(s, dirns, piece)
        if group == 2:
            for piece in range(2):
                ring_step(2, (0, 1), piece)

    def z_total(piece):
        for dirn in range(2):
            z_copy(dirn, 3, piece).wait_recv()
        at = plane(piece)
        return mine[at, z] + fromsib[at, z] + zr[0, 3, piece].astype(F32) + zr[1, 3, piece].astype(F32)

    pair = rcopy(xs, xrv, hss, hrs, partner)
    xs[...] = z_total(0)
    pair.start()
    own_sum = z_total(1)
    pair.wait_recv()
    summed = own_sum + xrv[...]
    pseudo = ow[...] - summed / 32
    momentum = nesterov * om[...] + pseudo
    outer = ow[...] - outer_rate * (pseudo + nesterov * momentum)
    nm[...] = momentum
    no[...] = outer

    share = outer.astype(BF16)
    for part in range(2):
        nw[part, h, z, core] = share[:, part * HALF:(part + 1) * HALF]

    def spread(part, ph, pz, ss, rs, dev):
        at = nw.at[part, ph, pz, core]
        return rcopy(at, at, ss, rs, dev)

    def ring_copy(part, dirn, d, piece):
        pz = (z + (8 - d if dirn == 0 else d)) % 8
        return spread(part, piece, pz, ass_.at[part, dirn, d, piece], ars.at[part, dirn, d, piece], zdev[dirn])

    def ring_first(part, ph):
        for dirn in range(2):
            spread(part, ph, z, ass_.at[part, dirn, 0, ph], ars.at[part, dirn, 0, ph], zdev[dirn]).start()

    def sib_spread(part, ph, pz):
        return spread(part, ph, pz, sss.at[part, ph, pz], srs.at[part, ph, pz], sibling)

    def cross(part):
        return spread(part, h, z, axs.at[part], axr.at[part], partner)

    for part in range(2):
        cross(part).start()
    for part in range(2):
        ring_first(part, h)
        sib_spread(part, h, z).start()
    for n in range(3, 11):
        na_copy(n).start()
    for part in range(2):
        cross(part).wait_recv()
        ring_first(part, 1 - h)
        sib_spread(part, 1 - h, z).start()
    for y in range(4):
        gx_copy(2, y).wait_recv()

    def late_step(k, c):
        igs[at_rows(768 + k * TOK, TOK, TOK)] = grad_cols(glo[at_rows(k * TOK, TOK, TOK)])
        return c

    lax.fori_loop(0, 2, late_step, 0)
    for n in range(7, 11):
        ig_copy(n).start()
    ig_own = pltpu.make_async_copy(igs.at[at_rows(yy * TOK, TOK, TOK)], ig.at[:, cols(f)], loc.at[3])
    ig_own.start()

    def ring_arrival(part, d):
        for piece in range(2):
            for dirn in range(2):
                if d == 3 and piece != dirn:
                    continue
                ring_copy(part, dirn, d, piece).wait_recv()
                if d < (3 if piece == dirn else 2):
                    ring_copy(part, dirn, d + 1, piece).start()
                sib_spread(part, piece, (z + (7 - d if dirn == 0 else d + 1)) % 8).start()

    for d in range(4):
        for part in range(2):
            ring_arrival(part, d)

    def kx_copy(q, side):
        return rcopy(ksx.at[q, side], krx.at[q, side], kxs.at[q, side], kxr.at[q, side], high(0) if side else low(0))

    def ky_copy(q, n):
        dy = (1, 3, 2)[n]
        return rcopy(ksy.at[q, (yy + dy) % 4], kry.at[q, yy], kys.at[q, n], kyr.at[q, n], same(dy))

    def weight(q):
        return nw[q // 2, :, :, :, :, pl.ds(q % 2 * QUAD, QUAD)].reshape(BLK, QUAD)

    own[1].wait()
    for n in range(11):
        na_copy(n).wait_recv()
    for q in range(4):
        if q % 2 == 0:
            for ph in range(2):
                for pz in range(8):
                    sib_spread(q // 2, ph, pz).wait_recv()
        for side in range(2):
            ksx[q, side] = jnp.dot(nar[pl.ds(512 + side * 256, 256)], weight(q), preferred_element_type=F32).astype(BF16)
            kx_copy(q, side).start()
    for q in range(4):
        acc[q] = jnp.dot(nar[pl.ds(0, 512)], weight(q), preferred_element_type=F32).reshape(4, TOK, QUAD)
    for q in range(4):
        for side in range(2):
            kx_copy(q, side).wait_recv()

        def pair_sum(y):
            other = jnp.concatenate([krx[q, 0, at_rows(y * 64, 64, 64)], krx[q, 1, at_rows(y * 64, 64, 64)]], axis=0)
            return acc[q, y] + other.astype(F32)

        for n in range(3):
            to = (yy + (1, 3, 2)[n]) % 4
            ksy[q, to] = pair_sum(to).astype(BF16)
            ky_copy(q, n).start()
        acc[q, yy] = pair_sum(yy)
    for q in range(4):
        total = acc[q, yy]
        for n in range(3):
            ky_copy(q, n).wait_recv()
            total = total + kry[q, (yy + 4 - (1, 3, 2)[n]) % 4].astype(F32)
        nk[:, pl.ds(q * QUAD, QUAD)] = total.astype(BF16)

    for n in range(11):
        ig_copy(n).wait_recv()
    ig_own.wait()
    for n in range(11):
        ig_copy(n).wait_send()
        na_copy(n).wait_send()
    for n in range(2):
        gy_copy(n).wait_send()
        gz_copy(n).wait_send()
    for n in range(3):
        for y in range(4):
            gx_copy(n, y).wait_send()

    def drain_x(b, c):
        for n in range(11):
            x_copy(b, n).wait_send()
        return c

    lax.fori_loop(0, 8, drain_x, 0)
    for b in range(8):
        sib_copy(b).wait_send()
    for s in range(4):
        for piece in range(2):
            for dirn in range(2):
                if used(dirn, s, piece):
                    z_copy(dirn, s, piece).wait_send()
    pair.wait_send()
    for part in range(2):
        cross(part).wait_send()
        for d in range(4):
            for piece in range(2):
                for dirn in range(2):
                    if d < 3 or piece == dirn:
                        ring_copy(part, dirn, d, piece).wait_send()
        for ph in range(2):
            for pz in range(8):
                sib_spread(part, ph, pz).wait_send()
    for q in range(4):
        for side in range(2):
            kx_copy(q, side).wait_send()
        for n in range(3):
            ky_copy(q, n).wait_send()


def move(*refs):
    sources, targets, (wide, keys, outer, momentum, got, put) = refs[:4], refs[4:8], refs[8:]
    steps = []
    for n in range(8):
        at = (slice(None), pl.ds(n * BLK, BLK))
        steps.append((sources[0].at[at], wide.at[at], targets[0].at[at]))
    for source, between, target in zip(sources[1:], (keys, outer, momentum), targets[1:]):
        steps.append((source, between, target))
    into = [pltpu.make_async_copy(a, b, got.at[n]) for n, (a, b, _) in enumerate(steps)]
    out = [pltpu.make_async_copy(b, c, put.at[n]) for n, (_, b, c) in enumerate(steps)]
    for copy in into:
        copy.start()
    for n, copy in enumerate(into):
        copy.wait()
        out[n].start()
    for copy in out:
        copy.wait()


def hand_over(arrays):
    hb = pl.BlockSpec(memory_space=pl.ANY)
    return pl.pallas_call(
        move,
        out_shape=tuple(jax.ShapeDtypeStruct(a.shape, a.dtype) for a in arrays),
        in_specs=[hb] * 4,
        out_specs=(hb,) * 4,
        scratch_shapes=[pltpu.VMEM(a.shape, a.dtype) for a in arrays]
        + [pltpu.SemaphoreType.DMA((11,)), pltpu.SemaphoreType.DMA((11,))],
    )(*arrays)


def local(activations, cotangent, inner_weight, outer_weight, outer_momentum, next_activations):
    vm = pl.BlockSpec(memory_space=pltpu.VMEM)
    hb = pl.BlockSpec(memory_space=pl.ANY)
    dma = pltpu.SemaphoreType.DMA
    ig, nk, no, nm = pl.pallas_call(
        kernel,
        out_shape=(
            jax.ShapeDtypeStruct((TOK, 8 * BLK), BF16),
            jax.ShapeDtypeStruct((TOK, KV), BF16),
            jax.ShapeDtypeStruct((SH, KV), F32),
            jax.ShapeDtypeStruct((SH, KV), F32),
        ),
        in_specs=[hb, hb, hb, vm, vm, hb],
        out_specs=(hb, vm, vm, vm),
        scratch_shapes=[
            pltpu.VMEM((BLK, KV), BF16),
            pltpu.VMEM((8 * TOK, BLK), BF16),
            pltpu.VMEM((8 * TOK, KV), BF16),
            pltpu.VMEM((256, KV), BF16),
            pltpu.VMEM((8 * TOK, BLK), BF16),
            pltpu.VMEM((8 * TOK, BLK), BF16),
            pltpu.VMEM((2, 8, SH, KV), F32),
            pltpu.VMEM((2, 8, SH, KV), F32),
            pltpu.VMEM((2, 8, SH, KV), F32),
            pltpu.VMEM((2, 4, 2, SH, KV), BF16),
            pltpu.VMEM((2, 4, 2, SH, KV), BF16),
            pltpu.VMEM((SH, KV), F32),
            pltpu.VMEM((SH, KV), F32),
            pltpu.VMEM((2, 2, 8, 2, SH, HALF), BF16),
            pltpu.VMEM((4, 2, 256, QUAD), BF16),
            pltpu.VMEM((4, 2, 256, QUAD), BF16),
            pltpu.VMEM((4, 4, TOK, QUAD), BF16),
            pltpu.VMEM((4, 4, TOK, QUAD), BF16),
            pltpu.VMEM((4, 4, TOK, QUAD), F32),
            dma((5,)),
            dma((4,)), dma((4,)),
            dma((3, 4)), dma((3, 4)),
            dma((8, 11)), dma((8, 11)),
            dma((11,)), dma((11,)),
            dma((11,)), dma((11,)),
            dma((4, 2)), dma((4, 2)),
            dma((4, 3)), dma((4, 3)),
            dma((8,)), dma((8,)),
            dma((2, 4, 2)), dma((2, 4, 2)),
            dma, dma,
            dma((2, 2, 4, 2)), dma((2, 2, 4, 2)),
            dma((2,)), dma((2,)),
            dma((2, 2, 8)), dma((2, 2, 8)),
        ],
        compiler_params=pltpu.CompilerParams(collective_id=0, has_side_effects=True, vmem_limit_bytes=60 * 1024 * 1024),
    )(activations, cotangent, inner_weight, outer_weight, outer_momentum, next_activations)
    return hand_over((ig, nk, no, nm))


def solution(mesh):
    in_specs = (
        P(("island", "fsdp"), None),
        P(("island", "fsdp"), None),
        P("island", "fsdp", None),
        P(("fsdp", "island"), None),
        P(("fsdp", "island"), None),
        P(("island", "fsdp"), None),
    )
    out_specs = (
        P(("island", "fsdp"), None),
        P(("island", "fsdp"), None),
        P(("fsdp", "island"), None),
        P(("fsdp", "island"), None),
    )
    return jax.shard_map(local, mesh=mesh, in_specs=in_specs, out_specs=out_specs, check_vma=False)
```
